32 devices in a mesh: groups: 2 (over y), seq: 4 (over z), head: 2 (over x), dp: 2 (over core).
Axes of the slice: x: 2, y: 2, z: 4, core: 2. Of those that a mesh axis runs over, the one named last changes fastest.
Arguments:
- queries: bfloat16 [4, 512, 2560], P(('groups', 'dp'), 'seq', 'head'), parts along dimension 0, may hold values from -25 to 25
- keys: bfloat16 [4, 512, 2560], P(('groups', 'dp'), 'seq', 'head'), parts along dimension 0, may hold values from -25 to 25
- values: bfloat16 [4, 512, 2560], P(('groups', 'dp'), 'seq', 'head'), parts along dimension 0, may hold values from -6 to 6
- out_grad: bfloat16 [4, 512, 2560], P(('groups', 'dp'), 'seq'), parts along dimension 0, may hold values from -6 to 6
- out_weight: bfloat16 [2560, 2560], P('dp', 'head'), may hold values from -0.125 to 0.125
- pattern: int32 [4, 2], P('seq'), may hold values from 0 to 1, as said below
- valid: int32 [4, 4], P(('groups', 'dp'), 'seq'), parts along dimension 0, may hold values from 64 to 128, as said below
Outputs:
- query_grad: bfloat16 [4, 512, 2560], P(('groups', 'dp'), 'seq', 'head'), parts along dimension 0
- key_grad: bfloat16 [4, 512, 2560], P(('groups', 'dp'), 'seq', 'head'), parts along dimension 0
- value_grad: bfloat16 [4, 512, 2560], P(('groups', 'dp'), 'seq', 'head'), parts along dimension 0
- weight_grad: float32 [5120, 2560], P(('groups', 'seq', 'dp'), 'head'), parts along dimension 0
The draws below stay inside these ranges and needn't reach their ends.
There are 2 independent parts, one for each index of `groups`. The reference program is written for one: setup_inputs(seed, part) draws one part's arguments, and reference() takes and returns one part's arrays. A program takes and returns all parts, laid end to end along the dimension named above; an argument that names none is the same for every part. Nothing has to cross between parts.
Inputs may be any that keep to these rules, and one draw needn't show every extreme that they name: pattern[i, k] is 0 where i < 2^k. `valid`: some block of each draw holds 128 real tokens.
All inputs are finite; a program needn't handle non-finite values.
Results may differ from the reference program's by a relative error of at most 0.02.
Values may be sent and summed in bfloat16 or wider, within the bound.
A program may use at most 64 MiB of HBM per device.

```python
import jax
import jax.numpy as jnp
from jax import lax

HEAD = 128
HEADS = 20
D = 2560
TOK_DEV = 128
HD = 2560
NB = 4
TOKENS = 512
CLIPS = 2
LEVELS = 2


def draw_queries(key, part):
    sample = jnp.clip(jax.random.normal(jax.random.fold_in(key, 1), (CLIPS, TOKENS, HEADS, HEAD), jnp.float32), -4.5, 4.5)
    return sample.reshape(CLIPS, TOKENS, HEADS * HEAD).astype(jnp.bfloat16)


def draw_keys(key, part):
    sample = jnp.clip(jax.random.normal(jax.random.fold_in(key, 2), (CLIPS, TOKENS, HEADS, HEAD), jnp.float32), -4.5, 4.5)
    return sample.reshape(CLIPS, TOKENS, HEADS * HEAD).astype(jnp.bfloat16)


def draw_pattern(key, part):
    coin_draw = jax.random.randint(jax.random.fold_in(key, 3), (NB, LEVELS), 0, 4)
    block_index = jnp.arange(NB, dtype=jnp.int32)[:, None]
    distance = jnp.left_shift(jnp.int32(1), jnp.arange(LEVELS, dtype=jnp.int32))[None, :]
    return jnp.where((coin_draw > 0) & (block_index >= distance), 1, 0).astype(jnp.int32)


def draw_valid(key, part):
    counts = jax.random.randint(jax.random.fold_in(key, 5), (CLIPS * NB,), TOK_DEV // 2, TOK_DEV + 1)
    full_index = jax.random.randint(jax.random.fold_in(key, 6), (), 0, CLIPS * NB)
    counts = jnp.where(jnp.arange(CLIPS * NB) == full_index, TOK_DEV, counts)
    return counts.reshape(CLIPS, NB).astype(jnp.int32)


def raised(values, key, source, target, shards_of, factor):
    owner, partner = [(jnp.arange(values.shape[dim]) // (values.shape[dim] // shards_of)).reshape([-1 if axis == dim else 1 for axis in range(values.ndim)]) for dim in (source, target)]
    chosen = jax.random.permutation(key, shards_of)[partner]
    strong = (owner == chosen) | (owner == (partner + shards_of // 2) % shards_of)
    return jnp.where(strong, factor * values, values)


def level_of(key, dims, cuts, smallest, high):
    def one(axis_at, blocks):
        heights = jax.random.uniform(jax.random.fold_in(jax.random.fold_in(key, 6), axis_at), (blocks,), jnp.float32, smallest / len(cuts), high / len(cuts))
        return jnp.repeat(jnp.exp(heights), dims[axis_at] // blocks).reshape((-1,) + (1,) * (len(dims) - axis_at - 1))

    factor_of = one(*cuts[0])
    for cut in cuts[1:]:
        factor_of = factor_of * one(*cut)
    return factor_of


def bell_draw(rng, dims, deviation, most, split=(), kind=jnp.bfloat16):
    entries = deviation * jax.random.normal(rng, dims, jnp.float32)
    if split:
        entries = entries * level_of(rng, dims, split, -0.22, 0.18)
    return jnp.clip(entries, -most, most).astype(kind)


def heavy_noise(own_key, shape, width, reach, pieces, heavy, held_as=jnp.bfloat16):
    entries = width * jax.random.normal(own_key, shape, jnp.float32)
    if pieces:
        entries = entries * level_of(own_key, shape, pieces, -0.22, 0.18)
    return jnp.clip(raised(entries, jax.random.fold_in(own_key, 3), *heavy), -reach, reach).astype(held_as)


def setup_inputs(seed: int = 0, part: int = 0) -> dict:
    streams_of = jax.random.split(jax.random.key(seed), 8)
    own_keys = jax.random.split(jax.random.fold_in(streams_of[7], part), 8)
    queries = draw_queries(jax.random.fold_in(jax.random.fold_in(streams_of[7], part), 71), part)
    keys = draw_keys(jax.random.fold_in(jax.random.fold_in(streams_of[7], part), 71), part)
    values = bell_draw(own_keys[2], (CLIPS, TOKENS, HD), 1.0, 6.0, ((0, 2), (1, 4), (2, 2)))
    out_grad = heavy_noise(own_keys[3], (CLIPS, TOKENS, D), 1.0, 6.0, ((0, 2), (1, 4)), (1, 2, 4, 2.0))
    out_weight = bell_draw(streams_of[4], (D, HD), HD ** -0.5, 0.125, ((0, 2), (1, 2)))
    pattern = draw_pattern(jax.random.fold_in(streams_of[7], 71), part)
    valid = draw_valid(jax.random.fold_in(jax.random.fold_in(streams_of[7], part), 71), part)
    return dict(queries=queries, keys=keys, values=values, out_grad=out_grad, out_weight=out_weight, pattern=pattern, valid=valid)


head_scale = 0.08838834764831845
masked_score = -1.0e30


def rounded(values_in):
    return lax.optimization_barrier(values_in.astype(jnp.bfloat16)).astype(jnp.float32)


def masked_scores(query_block, key_block, key_count, allowed):
    scores = jnp.einsum("qhd,khd->hqk", query_block.astype(jnp.float32), key_block.astype(jnp.float32)) * head_scale
    visible = (jnp.arange(TOK_DEV, dtype=jnp.int32) < key_count) & (allowed > 0)
    return jnp.where(visible[None, None, :], scores, masked_score)


def clip_pass(queries, keys, values, out_grad, out_weight, pattern, valid):
    query_blocks = queries.reshape(NB, TOK_DEV, HEADS, HEAD)
    key_blocks = keys.reshape(NB, TOK_DEV, HEADS, HEAD)
    value_blocks = values.reshape(NB, TOK_DEV, HEADS, HEAD)
    grad_in = jnp.dot(out_grad, out_weight, preferred_element_type=jnp.float32).astype(jnp.bfloat16)
    grad_blocks = grad_in.reshape(NB, TOK_DEV, HEADS, HEAD)
    distances = [0] + [2 ** level_index for level_index in range(LEVELS)]

    def one_block(carry, block_index):
        key_total, value_total = carry
        query_block = query_blocks[block_index]
        sources = []
        for set_index, distance in enumerate(distances):
            source = jnp.maximum(block_index - distance, 0).astype(jnp.int32)
            if set_index == 0:
                allowed = jnp.int32(1)
            else:
                allowed = pattern[block_index, set_index - 1]
            sources.append((source, allowed))
        score_sets = [masked_scores(query_block, key_blocks[source], valid[source], allowed) for source, allowed in sources]
        row_max = jnp.max(score_sets[0], axis=-1)
        for scores in score_sets[1:]:
            row_max = jnp.maximum(row_max, jnp.max(scores, axis=-1))
        row_total = jnp.zeros_like(row_max)
        for scores in score_sets:
            row_total = row_total + jnp.sum(jnp.exp(scores - row_max[..., None]), axis=-1)
        log_total = row_max + jnp.log(row_total)
        prob_sets = [jnp.exp(scores - log_total[..., None]) for scores in score_sets]
        attended = jnp.zeros((TOK_DEV, HEADS, HEAD), jnp.float32)
        for source_pair, prob_set in zip(sources, prob_sets):
            attended = attended + jnp.einsum("hqk,khd->qhd", rounded(prob_set), value_blocks[source_pair[0]].astype(jnp.float32))
        attended = attended.astype(jnp.bfloat16)
        grad_block = grad_blocks[block_index].astype(jnp.float32)
        row_delta = jnp.einsum("qhd,qhd->hq", grad_block, attended.astype(jnp.float32))
        query_grad = jnp.zeros((TOK_DEV, HEADS, HEAD), jnp.float32)
        for source_pair, prob_set in zip(sources, prob_sets):
            source = source_pair[0]
            value_part = jnp.einsum("hqk,qhd->khd", rounded(prob_set), grad_block)
            prob_grad = jnp.einsum("qhd,khd->hqk", grad_block, value_blocks[source].astype(jnp.float32))
            score_grad = rounded(prob_set * (prob_grad - row_delta[..., None]))
            query_grad = query_grad + jnp.einsum("hqk,khd->qhd", score_grad, key_blocks[source].astype(jnp.float32)) * head_scale
            key_part = jnp.einsum("hqk,qhd->khd", score_grad, query_block.astype(jnp.float32)) * head_scale
            key_total = key_total.at[source].add(key_part)
            value_total = value_total.at[source].add(value_part)
        return (key_total, value_total), (query_grad.astype(jnp.bfloat16), attended)

    start_totals = (jnp.zeros((NB, TOK_DEV, HEADS, HEAD), jnp.float32), jnp.zeros((NB, TOK_DEV, HEADS, HEAD), jnp.float32))
    totals, block_outs = lax.scan(one_block, start_totals, jnp.arange(NB, dtype=jnp.int32))
    query_grad = block_outs[0].reshape(TOKENS, HD)
    attended_all = block_outs[1].reshape(NB, TOK_DEV, HD)
    key_grad = totals[0].astype(jnp.bfloat16).reshape(TOKENS, HD)
    value_grad = totals[1].astype(jnp.bfloat16).reshape(TOKENS, HD)
    out_blocks = out_grad.reshape(NB, TOK_DEV, D)

    def add_term(running, block_pair):
        block_term = jnp.dot(block_pair[0].T, block_pair[1], preferred_element_type=jnp.float32)
        return running + rounded(block_term), None

    weight_grad, unused = lax.scan(add_term, jnp.zeros((D, HD), jnp.float32), (out_blocks, attended_all))
    return query_grad, key_grad, value_grad, weight_grad


def reference(queries, keys, values, out_grad, out_weight, pattern, valid):
    results = [clip_pass(queries[clip_index], keys[clip_index], values[clip_index], out_grad[clip_index], out_weight, pattern, valid[clip_index]) for clip_index in range(CLIPS)]
    query_grad = jnp.stack([result[0] for result in results])
    key_grad = jnp.stack([result[1] for result in results])
    value_grad = jnp.stack([result[2] for result in results])
    weight_grad = results[0][3]
    for result in results[1:]:
        weight_grad = weight_grad + result[3]
    return (query_grad, key_grad, value_grad, weight_grad)
```

```python
import functools

import jax
import jax.numpy as jnp
from jax import lax
from jax.experimental import pallas as pl
from jax.experimental.pallas import tpu as pltpu
from jax.sharding import PartitionSpec as P

HEAD = 128


head_scale = 0.08838834764831845
masked_score = -1e30


def from_behind(value, axis, steps):
    count = lax.axis_size(axis)
    first, last = (max(0, -steps), min(count, count - steps))
    return lax.ppermute(value, axis, [(source, source + steps) for source in range(first, last)])


def split_heads(matrix):
    return matrix.reshape(matrix.shape[0], matrix.shape[1], -1, HEAD)


def local(queries, keys, values, out_grad, out_weight, pattern, valid):
    clip_count, row_count, width_dev = queries.shape
    levels = lax.axis_size("seq").bit_length() - 1
    positions = jnp.arange(row_count, dtype=jnp.int32)
    key_list = [keys]
    value_list = [values]
    visible_list = [positions[None, :] < valid]
    for level_index in range(levels):
        far_keys, far_values, far_valid = from_behind((keys, values, valid), "seq", 2**level_index)
        key_list.append(far_keys)
        value_list.append(far_values)
        visible_list.append((positions[None, :] < far_valid) & (pattern[0, level_index] > 0))
    key_heads = split_heads(jnp.concatenate(key_list, axis=1))
    value_heads = split_heads(jnp.concatenate(value_list, axis=1))
    visible = jnp.concatenate(visible_list, axis=1)
    query_heads = split_heads(queries)
    scores = (
        jnp.einsum("cqhd,ckhd->chqk", query_heads, key_heads, preferred_element_type=jnp.float32)
        * head_scale
    )
    scores = jnp.where(visible[:, None, None, :], scores, masked_score)
    row_max = jnp.max(scores, axis=-1, keepdims=True)
    log_total = row_max + jnp.log(jnp.sum(jnp.exp(scores - row_max), axis=-1, keepdims=True))
    probs_full = jnp.exp(scores - log_total)
    weights = probs_full.astype(jnp.bfloat16)
    attended = jnp.einsum(
        "chqk,ckhd->cqhd", weights, value_heads, preferred_element_type=jnp.float32
    ).astype(jnp.bfloat16)
    columns = out_grad
    grad_in = jnp.einsum(
        "cqe,eh->cqh",
        columns,
        lax.all_gather(out_weight, "dp", axis=0, tiled=True),
        preferred_element_type=jnp.float32,
    ).astype(jnp.bfloat16)
    grad_heads = split_heads(grad_in)
    row_delta = jnp.einsum(
        "cqhd,cqhd->chq", grad_heads.astype(jnp.float32), attended.astype(jnp.float32)
    )
    value_grad_all = jnp.einsum(
        "chqk,cqhd->ckhd", weights, grad_heads, preferred_element_type=jnp.float32
    )
    prob_grad = jnp.einsum(
        "cqhd,ckhd->chqk", grad_heads, value_heads, preferred_element_type=jnp.float32
    )
    score_grad = (probs_full * (prob_grad - row_delta[..., None])).astype(jnp.bfloat16)
    query_grad = (
        jnp.einsum("chqk,ckhd->cqhd", score_grad, key_heads, preferred_element_type=jnp.float32)
        * head_scale
    )
    key_grad_all = (
        jnp.einsum("chqk,cqhd->ckhd", score_grad, query_heads, preferred_element_type=jnp.float32)
        * head_scale
    )
    key_grad_all = key_grad_all.reshape(clip_count, -1, width_dev)
    value_grad_all = value_grad_all.reshape(clip_count, -1, width_dev)
    key_parts = [
        key_grad_all[:, set_index * row_count : (set_index + 1) * row_count]
        for set_index in range(levels + 1)
    ]
    value_parts = [
        value_grad_all[:, set_index * row_count : (set_index + 1) * row_count]
        for set_index in range(levels + 1)
    ]
    key_total = key_parts[0]
    value_total = value_parts[0]
    for level_index in range(levels):
        back_keys, back_values = (
            from_behind(
                key_parts[level_index + 1].astype(jnp.bfloat16), "seq", -(2**level_index)
            ).astype(jnp.float32),
            from_behind(
                value_parts[level_index + 1].astype(jnp.bfloat16), "seq", -(2**level_index)
            ).astype(jnp.float32),
        )
        key_total = key_total + back_keys
        value_total = value_total + back_values
    attended_rows = attended.reshape(clip_count, row_count, width_dev)
    columns = out_grad
    seq_total = lax.psum_scatter(
        jnp.einsum(
            "cqe,cqh->eh", columns, attended_rows, preferred_element_type=jnp.float32
        ).astype(jnp.bfloat16),
        "seq",
        scatter_dimension=0,
        tiled=True,
    )
    weight_grad = lax.psum_scatter(seq_total, "dp", scatter_dimension=0, tiled=True).astype(
        jnp.float32
    )
    query_out = query_grad.astype(jnp.bfloat16).reshape(clip_count, row_count, width_dev)
    return (
        query_out,
        key_total.astype(jnp.bfloat16),
        value_total.astype(jnp.bfloat16),
        weight_grad,
    )


MESH = pl.DeviceIdType.MESH
CHUNK = 2 * HEAD
F32 = jnp.float32
BF16 = jnp.bfloat16


def dot_nn(a, b):
    return lax.dot_general(a, b, (((1,), (0,)), ((), ())), preferred_element_type=F32)


def dot_nt(a, b):
    return lax.dot_general(a, b, (((1,), (1,)), ((), ())), preferred_element_type=F32)


def dot_tn(a, b):
    return lax.dot_general(a, b, (((0,), (0,)), ((), ())), preferred_element_type=F32)


def kernel(
    n,
    rows_out,
    valid_ref,
    pattern_hbm,
    q_hbm,
    k_hbm,
    v_hbm,
    og_hbm,
    w_hbm,
    dq_ref,
    dk_ref,
    dv_ref,
    wg_ref,
    q_ref,
    og_ref,
    w_ref,
    kv,
    counts,
    lhs,
    gacc,
    gsend,
    grecv,
    self_g,
    one_g,
    stage,
    back,
    att,
    cols_all,
    kv_send,
    kv_recv,
    count_send,
    count_recv,
    half_send,
    half_recv,
    g_send,
    g_recv,
    back_send,
    back_recv,
    att_send,
    att_recv,
    col_send,
    col_recv,
    cross_send,
    cross_recv,
    load_sem,
    pattern_ref,
):
    s = lax.axis_index("seq")
    d = lax.axis_index("dp")
    h = lax.axis_index("head")
    tok, width = q_ref.shape
    half = w_ref.shape[0]
    chunks = width // CHUNK
    wide = cols_all.shape[3]
    right, left, mate = {"seq": s + 1}, {"seq": s - 1}, {"dp": 1 - d}
    has_left, has_right = s >= 1, s < n - 1

    def remote(src, dst, send, recv, device):
        return pltpu.make_async_remote_copy(
            src_ref=src, dst_ref=dst, send_sem=send, recv_sem=recv, device_id=device, device_id_type=MESH
        )

    def cut(c):
        return pl.ds(c * CHUNK, CHUNK)

    def kv_copy(level, c):
        return remote(
            kv.at[:, pl.ds(level * tok, tok), cut(c)],
            kv.at[:, pl.ds((level + 1) * tok, tok), cut(c)],
            kv_send.at[level, c],
            kv_recv.at[level, c],
            right,
        )

    def count_copy(level):
        return remote(
            counts.at[level], counts.at[level + 1], count_send.at[level], count_recv.at[level], right
        )

    def half_copy():
        other = pl.multiple_of((1 - d) * half, half)
        return remote(og_ref.at[:, pl.ds(other, half)], lhs.at[1], half_send, half_recv, mate)

    def g_copy(c):
        return remote(gsend.at[:, cut(c)], grecv.at[:, cut(c)], g_send.at[c], g_recv.at[c], mate)

    def back_copy(which, c):
        return remote(
            stage.at[which, :, :, cut(c)],
            back.at[which, :, :, cut(c)],
            back_send.at[which, c],
            back_recv.at[which, c],
            left,
        )

    def att_copy(clip, origin, c, way):
        place = att.at[clip, origin, :, cut(c)]
        return remote(
            place, place, att_send.at[way, origin, c], att_recv.at[clip, origin, c], (right, left, mate)[way]
        )

    def col_start(seq, dp):
        return pl.multiple_of(seq * (2 * rows_out) + dp * (2 * rows_out - wide), HEAD)

    part_rows = tok // 2

    def rows_of(step, which):
        if step == 0:
            return pl.ds(0, tok)
        return pl.ds(pl.multiple_of(which * part_rows, part_rows), part_rows)

    def col_copy(step, flip):
        seq = lax.rem(s + step, n)
        dp = lax.rem(d + flip, 2)
        rows = rows_of(step, h)
        return remote(
            og_ref.at[rows, pl.ds(col_start(seq, dp), wide)],
            cols_all.at[d, s, rows, :],
            col_send.at[flip, step],
            col_recv.at[d, s],
            {"seq": seq, "dp": dp},
        )

    def col_arrived(step, flip):
        seq = lax.rem(s + step, n)
        dp = lax.rem(d + flip, 2)
        place = cols_all.at[dp, seq, rows_of(step, h), :]
        return remote(
            place, place, col_send.at[flip, step], col_recv.at[dp, seq], {"seq": seq, "dp": dp}
        )

    def cross_copy(step, flip, which):
        seq = lax.rem(s + step, n)
        dp = lax.rem(d + flip, 2)
        place = cols_all.at[dp, seq, rows_of(step, which), :]
        return remote(
            place, place, cross_send.at[flip, step], cross_recv.at[dp, seq], {"head": 1 - h}
        )

    loads = [
        pltpu.make_async_copy(k_hbm, kv.at[0, pl.ds(0, tok), :], load_sem.at[0]),
        pltpu.make_async_copy(v_hbm, kv.at[1, pl.ds(0, tok), :], load_sem.at[1]),
        pltpu.make_async_copy(og_hbm, og_ref, load_sem.at[2]),
        pltpu.make_async_copy(w_hbm, w_ref, load_sem.at[3]),
        pltpu.make_async_copy(q_hbm, q_ref, load_sem.at[4]),
        pltpu.make_async_copy(pattern_hbm, pattern_ref, load_sem.at[5]),
    ]

    barrier = pltpu.get_barrier_semaphore()
    others = [(step, flip) for step in range(n) for flip in range(2) if step or flip]
    for step, flip in others:
        pl.semaphore_signal(
            barrier,
            inc=1,
            device_id={"seq": lax.rem(s + step, n), "dp": lax.rem(d + flip, 2)},
            device_id_type=MESH,
        )
    pl.semaphore_signal(barrier, inc=1, device_id={"head": 1 - h}, device_id_type=MESH)
    for load in loads:
        load.start()
    counts[0] = jnp.full((8, 128), valid_ref[0, 0], jnp.int32)

    @pl.when(s < 1)
    def _():
        kv[:, pl.ds(tok, tok), :] = jnp.zeros((2, tok, width), BF16)
        counts[1] = jnp.zeros((8, 128), jnp.int32)

    @pl.when(s < 2)
    def _():
        kv[:, pl.ds(2 * tok, tok), :] = jnp.zeros((2, tok, width), BF16)
        counts[2] = jnp.zeros((8, 128), jnp.int32)

    @pl.when(jnp.logical_or(s < 1, s > n - 2))
    def _():
        back[0] = jnp.zeros((2, tok, width), BF16)

    @pl.when(s > n - 2)
    def _():
        back[1] = jnp.zeros((2, tok, width), BF16)

    loads[0].wait()
    loads[1].wait()
    pl.semaphore_wait(barrier, len(others) + 1)

    @pl.when(has_right)
    def _():
        count_copy(0).start()
        kv_copy(0, 0).start()
        kv_copy(0, 1).start()

    loads[2].wait()
    half_copy().start()

    for step, flip in others:

        @pl.when(s + step >= n)
        def _(step=step, flip=flip):
            col_copy(step, flip).start()

    col_copy(0, 1).start()
    lhs[0] = og_ref[:, pl.ds(pl.multiple_of(d * half, half), half)]
    cols_all[d, s] = og_ref[:, pl.ds(col_start(s, d), wide)]

    @pl.when(has_left)
    def _():
        count_copy(0).wait_recv()

    @pl.when(jnp.logical_and(has_left, has_right))
    def _():
        count_copy(1).start()

    loads[3].wait()
    half_copy().wait_recv()
    both = lhs[...].reshape(2 * tok, half)
    for c in range(chunks):
        part = dot_nn(both, w_ref[:, cut(c)])
        gacc[:, cut(c)] = part[:tok]
        gsend[:, cut(c)] = part[tok:].astype(BF16)
        g_copy(c).start()

    @pl.when(s >= 2)
    def _():
        count_copy(1).wait_recv()

    loads[5].wait()
    lane = lax.broadcasted_iota(jnp.int32, (1, 128), 1)
    seen = jnp.concatenate(
        [
            (lane < counts[0, 0:1, :]).astype(F32),
            jnp.where(pattern_ref[0, 0] > 0, (lane < counts[1, 0:1, :]).astype(F32), 0.0),
            jnp.where(pattern_ref[0, 1] > 0, (lane < counts[2, 0:1, :]).astype(F32), 0.0),
        ],
        axis=1,
    )
    visible = jnp.broadcast_to(seen, (tok, 3 * tok)) > 0.5

    loads[4].wait()

    def attend(c):
        g_copy(c).wait_recv()
        g_chunk = (gacc[:, cut(c)] + grecv[:, cut(c)].astype(F32)).astype(BF16)
        for inner in range(CHUNK // HEAD):
            hs = pl.ds(c * CHUNK + inner * HEAD, HEAD)
            q, k, v = q_ref[:, hs], kv[0, :, hs], kv[1, :, hs]
            g = g_chunk[:, inner * HEAD : (inner + 1) * HEAD]
            scores = jnp.where(visible, dot_nt(q, k) * head_scale, masked_score)
            top = jnp.max(scores, axis=1, keepdims=True)
            raised = jnp.exp(scores - top)
            probs = raised * (1.0 / jnp.sum(raised, axis=1, keepdims=True))
            weights = probs.astype(BF16)
            attended = dot_nn(weights, v).astype(BF16)
            att[d, s, :, hs] = attended
            delta = jnp.sum(g.astype(F32) * attended.astype(F32), axis=1, keepdims=True)
            score_grad = (probs * (dot_nt(g, v) - delta)).astype(BF16)
            dq_ref[:, hs] = (dot_nn(score_grad, k) * head_scale).astype(BF16)
            dk = dot_tn(score_grad, q) * head_scale
            dv = dot_tn(weights, g)
            for at, grad in ((0, dk), (1, dv)):
                self_g[at, :, hs] = grad[:tok]
                one_g[at, :, hs] = grad[tok : 2 * tok]
                stage[0, at, :, hs] = grad[2 * tok :].astype(BF16)

    def relay_grads(c):
        @pl.when(jnp.logical_and(has_left, has_right))
        def _():
            back_copy(0, c).wait_recv()

        @pl.when(has_left)
        def _():
            stage[1, :, :, cut(c)] = (
                one_g[:, :, cut(c)] + back[0, :, :, cut(c)].astype(F32)
            ).astype(BF16)
            back_copy(1, c).start()

    def finish_grads(c):
        @pl.when(has_right)
        def _():
            back_copy(1, c).wait_recv()

        total = self_g[:, :, cut(c)] + back[1, :, :, cut(c)].astype(F32)
        dk_ref[:, cut(c)] = total[0].astype(BF16)
        dv_ref[:, cut(c)] = total[1].astype(BF16)

    def relay_right(t, c):
        @pl.when(s - t >= 0)
        def _():
            att_copy(d, s - t, c, 0).wait_recv()
            att_copy(d, s - t, c, 2).start()

            @pl.when(has_right)
            def _():
                att_copy(d, s - t, c, 0).start()

    def relay_left(t, c):
        @pl.when(s + t < n)
        def _():
            att_copy(d, s + t, c, 1).wait_recv()
            att_copy(d, s + t, c, 2).start()

            @pl.when(has_left)
            def _():
                att_copy(d, s + t, c, 1).start()

    def weigh(c):
        for origin in range(n):
            att_copy(1 - d, origin, c, 2).wait_recv()
        full = dot_tn(
            cols_all[...].reshape(2 * n * tok, wide), att[:, :, :, cut(c)].reshape(2 * n * tok, CHUNK)
        )

        @pl.when(d == 0)
        def _():
            wg_ref[:, cut(c)] = full[:rows_out]

        @pl.when(d == 1)
        def _():
            wg_ref[:, cut(c)] = full[wide - rows_out :]

    for c in range(chunks + n + 2):
        if c < chunks:

            @pl.when(has_left)
            def _(c=c):
                kv_copy(0, c).wait_recv()

            @pl.when(jnp.logical_and(has_left, has_right))
            def _(c=c):
                kv_copy(1, c).start()

            if c + 2 < chunks:

                @pl.when(has_right)
                def _(c=c):
                    kv_copy(0, c + 2).start()

            @pl.when(s >= 2)
            def _(c=c):
                kv_copy(1, c).wait_recv()

            attend(c)

            @pl.when(s >= 2)
            def _(c=c):
                back_copy(0, c).start()

            @pl.when(has_left)
            def _(c=c):
                att_copy(d, s, c, 1).start()

            att_copy(d, s, c, 2).start()
        if c == chunks - 1:
            for step, flip in others:
                if step:

                    @pl.when(s + step < n)
                    def _(step=step, flip=flip):
                        col_copy(step, flip).start()

        if 2 <= c < chunks + 2:

            @pl.when(has_right)
            def _(c=c):
                att_copy(d, s, c - 2, 0).start()

        if 0 <= c - 2 < chunks:
            relay_grads(c - 2)
        for t in range(1, n):
            if 0 <= c - t < chunks:
                relay_left(t, c - t)
            if 0 <= c - t - 2 < chunks:
                relay_right(t, c - t - 2)
        if 0 <= c - 4 < chunks:
            finish_grads(c - 4)
        if c in (2, chunks):
            for step, flip in others:
                if step:

                    @pl.when(s + step < n if c == 2 else s + step >= n)
                    def _(step=step, flip=flip):
                        col_arrived(step, flip).wait_recv()
                        cross_copy(step, flip, h).start()

        if c == chunks:
            col_arrived(0, 1).wait_recv()
        if c == chunks + 1:
            for step, flip in others:
                if step:
                    cross_copy(step, flip, 1 - h).wait_recv()
        if c > chunks + 1 and c - chunks - 2 < chunks - 1:
            weigh(c - chunks - 2)
    weigh(chunks - 1)

    half_copy().wait_send()
    for step, flip in others:
        col_copy(step, flip).wait_send()
        if step:
            cross_copy(step, flip, h).wait_send()

    @pl.when(has_right)
    def _():
        count_copy(0).wait_send()

    @pl.when(jnp.logical_and(has_left, has_right))
    def _():
        count_copy(1).wait_send()

    for c in range(chunks):
        g_copy(c).wait_send()

        @pl.when(has_right)
        def _(c=c):
            kv_copy(0, c).wait_send()

        @pl.when(jnp.logical_and(has_left, has_right))
        def _(c=c):
            kv_copy(1, c).wait_send()

        @pl.when(s >= 2)
        def _(c=c):
            back_copy(0, c).wait_send()

        @pl.when(has_left)
        def _(c=c):
            back_copy(1, c).wait_send()

        for origin in range(n):
            att_copy(d, origin, c, 2).wait_send()

            @pl.when(jnp.logical_and(origin <= s, has_right))
            def _(c=c, origin=origin):
                att_copy(d, origin, c, 0).wait_send()

            @pl.when(jnp.logical_and(origin >= s, has_left))
            def _(c=c, origin=origin):
                att_copy(d, origin, c, 1).wait_send()


def out_kernel(*refs):
    count = len(refs) // 2
    sems = refs[-1]
    copies = [pltpu.make_async_copy(refs[i], refs[count + i], sems.at[i]) for i in range(count)]
    for copy in copies:
        copy.start()
    for copy in copies:
        copy.wait()


def write_out(arrays):
    return pl.pallas_call(
        out_kernel,
        out_shape=tuple(jax.ShapeDtypeStruct(a.shape, a.dtype) for a in arrays),
        in_specs=[pl.BlockSpec(memory_space=pltpu.VMEM)] * len(arrays),
        out_specs=(pl.BlockSpec(memory_space=pltpu.HBM),) * len(arrays),
        scratch_shapes=[pltpu.SemaphoreType.DMA((len(arrays),))],
        compiler_params=pltpu.CompilerParams(vmem_limit_bytes=4 * 1024 * 1024),
    )(*arrays)


def fused(n, rows_out, queries, keys, values, out_grad, out_weight, pattern, valid):
    _, tok, width = queries.shape
    half = out_weight.shape[0]
    chunks = width // CHUNK
    wide = -(-rows_out // HEAD) * HEAD
    vmem = pl.BlockSpec(memory_space=pltpu.VMEM)
    hbm = pl.BlockSpec(memory_space=pltpu.HBM)
    smem = pl.BlockSpec(memory_space=pltpu.SMEM)
    dma = pltpu.SemaphoreType.DMA
    rows_bf = jax.ShapeDtypeStruct((tok, width), BF16)
    outs = pl.pallas_call(
        functools.partial(kernel, n, rows_out),
        out_shape=(rows_bf, rows_bf, rows_bf, jax.ShapeDtypeStruct((rows_out, width), F32)),
        in_specs=[smem] + [hbm] * 6,
        out_specs=(vmem,) * 4,
        scratch_shapes=[
            pltpu.VMEM((tok, width), BF16),
            pltpu.VMEM((tok, out_grad.shape[2]), BF16),
            pltpu.VMEM((half, width), BF16),
            pltpu.VMEM((2, 3 * tok, width), BF16),
            pltpu.VMEM((3, 8, 128), jnp.int32),
            pltpu.VMEM((2, tok, half), BF16),
            pltpu.VMEM((tok, width), F32),
            pltpu.VMEM((tok, width), BF16),
            pltpu.VMEM((tok, width), BF16),
            pltpu.VMEM((2, tok, width), F32),
            pltpu.VMEM((2, tok, width), F32),
            pltpu.VMEM((2, 2, tok, width), BF16),
            pltpu.VMEM((2, 2, tok, width), BF16),
            pltpu.VMEM((2, n, tok, width), BF16),
            pltpu.VMEM((2, n, tok, wide), BF16),
            dma((2, chunks)),
            dma((2, chunks)),
            dma((2,)),
            dma((2,)),
            dma,
            dma,
            dma((chunks,)),
            dma((chunks,)),
            dma((2, chunks)),
            dma((2, chunks)),
            dma((3, n, chunks)),
            dma((2, n, chunks)),
            dma((2, n)),
            dma((2, n)),
            dma((2, n)),
            dma((2, n)),
            dma((6,)),
            pltpu.SMEM((1, 2), jnp.int32),
        ],
        compiler_params=pltpu.CompilerParams(
            collective_id=0, has_side_effects=True, vmem_limit_bytes=50 * 1024 * 1024
        ),
    )(valid, *[pltpu.with_memory_space_constraint(a, pltpu.HBM) for a in (pattern, queries[0], keys[0], values[0], out_grad[0], out_weight)])
    outs = write_out(outs)
    return outs[0][None], outs[1][None], outs[2][None], outs[3]


def fused_local(queries, keys, values, out_grad, out_weight, pattern, valid):
    n = lax.axis_size("seq")
    rows_out = out_grad.shape[2] // (2 * n)
    return fused(n, rows_out, queries, keys, values, out_grad, out_weight, pattern, valid)


def solution(mesh):
    n = mesh.shape["seq"]
    body = local
    if n == 4 and mesh.shape["dp"] == 2 and mesh.shape["head"] == 2:
        body = fused_local
    return jax.shard_map(
        body,
        mesh=mesh,
        in_specs=(
            P(("groups", "dp"), "seq", "head"),
            P(("groups", "dp"), "seq", "head"),
            P(("groups", "dp"), "seq", "head"),
            P(("groups", "dp"), "seq", None),
            P("dp", "head"),
            P("seq", None),
            P(("groups", "dp"), "seq"),
        ),
        out_specs=(
            P(("groups", "dp"), "seq", "head"),
            P(("groups", "dp"), "seq", "head"),
            P(("groups", "dp"), "seq", "head"),
            P(("groups", "seq", "dp"), "head"),
        ),
        check_vma=False,
    )
```

```python
import functools

import jax
import jax.numpy as jnp
from jax import lax
from jax.experimental import pallas as pl
from jax.experimental.pallas import tpu as pltpu
from jax.sharding import PartitionSpec as P

HEAD = 128


head_scale = 0.08838834764831845
masked_score = -1e30


def from_behind(value, axis, steps):
    count = lax.axis_size(axis)
    first, last = (max(0, -steps), min(count, count - steps))
    return lax.ppermute(value, axis, [(source, source + steps) for source in range(first, last)])


def split_heads(matrix):
    return matrix.reshape(matrix.shape[0], matrix.shape[1], -1, HEAD)


def local(queries, keys, values, out_grad, out_weight, pattern, valid):
    clip_count, row_count, width_dev = queries.shape
    levels = lax.axis_size("seq").bit_length() - 1
    positions = jnp.arange(row_count, dtype=jnp.int32)
    key_list = [keys]
    value_list = [values]
    visible_list = [positions[None, :] < valid]
    for level_index in range(levels):
        far_keys, far_values, far_valid = from_behind((keys, values, valid), "seq", 2**level_index)
        key_list.append(far_keys)
        value_list.append(far_values)
        visible_list.append((positions[None, :] < far_valid) & (pattern[0, level_index] > 0))
    key_heads = split_heads(jnp.concatenate(key_list, axis=1))
    value_heads = split_heads(jnp.concatenate(value_list, axis=1))
    visible = jnp.concatenate(visible_list, axis=1)
    query_heads = split_heads(queries)
    scores = (
        jnp.einsum("cqhd,ckhd->chqk", query_heads, key_heads, preferred_element_type=jnp.float32)
        * head_scale
    )
    scores = jnp.where(visible[:, None, None, :], scores, masked_score)
    row_max = jnp.max(scores, axis=-1, keepdims=True)
    log_total = row_max + jnp.log(jnp.sum(jnp.exp(scores - row_max), axis=-1, keepdims=True))
    probs_full = jnp.exp(scores - log_total)
    weights = probs_full.astype(jnp.bfloat16)
    attended = jnp.einsum(
        "chqk,ckhd->cqhd", weights, value_heads, preferred_element_type=jnp.float32
    ).astype(jnp.bfloat16)
    columns = out_grad
    grad_in = jnp.einsum(
        "cqe,eh->cqh",
        columns,
        lax.all_gather(out_weight, "dp", axis=0, tiled=True),
        preferred_element_type=jnp.float32,
    ).astype(jnp.bfloat16)
    grad_heads = split_heads(grad_in)
    row_delta = jnp.einsum(
        "cqhd,cqhd->chq", grad_heads.astype(jnp.float32), attended.astype(jnp.float32)
    )
    value_grad_all = jnp.einsum(
        "chqk,cqhd->ckhd", weights, grad_heads, preferred_element_type=jnp.float32
    )
    prob_grad = jnp.einsum(
        "cqhd,ckhd->chqk", grad_heads, value_heads, preferred_element_type=jnp.float32
    )
    score_grad = (probs_full * (prob_grad - row_delta[..., None])).astype(jnp.bfloat16)
    query_grad = (
        jnp.einsum("chqk,ckhd->cqhd", score_grad, key_heads, preferred_element_type=jnp.float32)
        * head_scale
    )
    key_grad_all = (
        jnp.einsum("chqk,cqhd->ckhd", score_grad, query_heads, preferred_element_type=jnp.float32)
        * head_scale
    )
    key_grad_all = key_grad_all.reshape(clip_count, -1, width_dev)
    value_grad_all = value_grad_all.reshape(clip_count, -1, width_dev)
    key_parts = [
        key_grad_all[:, set_index * row_count : (set_index + 1) * row_count]
        for set_index in range(levels + 1)
    ]
    value_parts = [
        value_grad_all[:, set_index * row_count : (set_index + 1) * row_count]
        for set_index in range(levels + 1)
    ]
    key_total = key_parts[0]
    value_total = value_parts[0]
    for level_index in range(levels):
        back_keys, back_values = (
            from_behind(
                key_parts[level_index + 1].astype(jnp.bfloat16), "seq", -(2**level_index)
            ).astype(jnp.float32),
            from_behind(
                value_parts[level_index + 1].astype(jnp.bfloat16), "seq", -(2**level_index)
            ).astype(jnp.float32),
        )
        key_total = key_total + back_keys
        value_total = value_total + back_values
    attended_rows = attended.reshape(clip_count, row_count, width_dev)
    columns = out_grad
    seq_total = lax.psum_scatter(
        jnp.einsum(
            "cqe,cqh->eh", columns, attended_rows, preferred_element_type=jnp.float32
        ).astype(jnp.bfloat16),
        "seq",
        scatter_dimension=0,
        tiled=True,
    )
    weight_grad = lax.psum_scatter(seq_total, "dp", scatter_dimension=0, tiled=True).astype(
        jnp.float32
    )
    query_out = query_grad.astype(jnp.bfloat16).reshape(clip_count, row_count, width_dev)
    return (
        query_out,
        key_total.astype(jnp.bfloat16),
        value_total.astype(jnp.bfloat16),
        weight_grad,
    )


MESH = pl.DeviceIdType.MESH
F32 = jnp.float32
BF16 = jnp.bfloat16
GRAD_CHUNK = 2 * HEAD


def dot_nn(a, b):
    return lax.dot_general(a, b, (((1,), (0,)), ((), ())), preferred_element_type=F32)


def dot_nt(a, b):
    return lax.dot_general(a, b, (((1,), (1,)), ((), ())), preferred_element_type=F32)


def dot_tn(a, b):
    return lax.dot_general(a, b, (((0,), (0,)), ((), ())), preferred_element_type=F32)


def attention(q, g, k, v, bias):
    scores = dot_nt(q, k) * head_scale + bias
    top = jnp.max(scores, axis=1, keepdims=True)
    raised = jnp.exp(scores - top)
    probs = raised * (1.0 / jnp.sum(raised, axis=1, keepdims=True))
    weights = probs.astype(BF16)
    attended = dot_nn(weights, v).astype(BF16)
    delta = jnp.sum(g.astype(F32) * attended.astype(F32), axis=1, keepdims=True)
    score_grad = (probs * (dot_nt(g, v) - delta)).astype(BF16)
    dq = (dot_nn(score_grad, k) * head_scale).astype(BF16)
    return attended, dq, dot_tn(score_grad, q) * head_scale, dot_tn(weights, g)


def kernel(
    rows_out,
    valid_ref,
    pattern_hbm,
    q_hbm,
    k_hbm,
    v_hbm,
    og_hbm,
    w_hbm,
    dq_ref,
    dk_ref,
    dv_ref,
    wg_ref,
    q_ref,
    og_ref,
    w_ref,
    kv,
    info,
    lhs,
    gacc,
    gsend,
    grecv,
    g_ref,
    acc,
    stage,
    back,
    outs,
    att,
    cols,
    pick,
    part,
    landed,
    pattern_ref,
    load_sem,
    info_send,
    info_recv,
    half_send,
    half_recv,
    gx_send,
    gx_recv,
    kv_send,
    kv_recv,
    edge_send,
    edge_recv,
    near_send,
    far_send,
    og_recv,
    x_send,
    x_recv,
    mate_send,
    mate_recv,
    att_send,
    att_recv,
    own_send,
    own_recv,
    fwd_send,
    fwd_recv,
    back_send,
    back_recv,
    res_send,
    res_recv,
    part_send,
    part_recv,
):
    s = lax.axis_index("seq")
    d = lax.axis_index("dp")
    h = lax.axis_index("head")
    tok, width = dq_ref.shape
    half = w_ref.shape[0]
    heads = width // HEAD
    seg = cols.shape[4]
    wide = pick.shape[4]
    mate = {"dp": 1 - d}
    part_rows = tok // 2

    def remote(src, dst, send, recv, device):
        return pltpu.make_async_remote_copy(
            src_ref=src, dst_ref=dst, send_sem=send, recv_sem=recv, device_id=device, device_id_type=MESH
        )

    def same(place, send, recv, device):
        return remote(place, place, send, recv, device)

    def cut(c):
        return pl.ds(c * HEAD, HEAD)

    def info_copy(block, target, slot):
        return same(info.at[block], info_send.at[slot], info_recv.at[block], {"seq": target})

    def half_copy():
        other = pl.multiple_of((1 - d) * half, half)
        return remote(og_ref.at[:, pl.ds(other, half)], lhs.at[1], half_send, half_recv, mate)

    def gx_copy(c):
        place = pl.ds(c * GRAD_CHUNK, GRAD_CHUNK)
        return remote(gsend.at[:, place], grecv.at[:, place], gx_send, gx_recv.at[c], mate)

    def kv_copy(which, c):
        first, count = ((0, 1), (1, 1), (0, 2))[which]
        place = kv.at[:, pl.ds(first * tok, count * tok), cut(c)]
        slot = 1 if which == 1 else 0
        return same(place, kv_send, kv_recv.at[slot, c], {"seq": 2})

    def edge_kv(block, c):
        place = kv.at[:, pl.ds(block * tok, tok), cut(c)]
        return same(place, edge_send.at[0], edge_recv.at[0, c], {"seq": 1 + block // 2})

    def edge_q(c):
        return remote(
            q_ref.at[0, :, cut(c)], q_ref.at[1, :, cut(c)], edge_send.at[1], edge_recv.at[1, c], {"seq": 2}
        )

    def edge_g(c):
        return remote(
            g_ref.at[0, :, cut(c)], g_ref.at[1, :, cut(c)], edge_send.at[2], edge_recv.at[2, c], {"seq": 2}
        )

    def edge_att(c):
        return same(att.at[d, 0, :, cut(c)], edge_send.at[1], edge_recv.at[1, c], {"seq": 1})

    def half_rows(row):
        return pl.ds(pl.multiple_of(row * part_rows, part_rows), part_rows)

    def own_columns(side, piece):
        return pl.ds((2 * side + (piece if side == 0 else 1 - piece)) * seg, seg)

    def og_copy(block, side, piece):
        sems = near_send if block // 2 == side else far_send
        return remote(
            og_ref.at[half_rows(h), own_columns(side, piece)],
            cols.at[d, piece, block, half_rows(h), :],
            sems,
            og_recv.at[block, piece],
            {"seq": 1 + side},
        )

    def x_copy(block, piece, mine):
        place = cols.at[d, piece, block, half_rows(h if mine else 1 - h), :]
        return same(place, x_send, x_recv.at[block, piece], {"head": 1 - h})

    def mate_copy(block, piece, clip):
        return same(cols.at[clip, piece, block], mate_send, mate_recv.at[block, piece], mate)

    def att_copy(pair, c):
        return same(
            att.at[d, pl.ds(2 * pair, 2), :, cut(c)], att_send, att_recv.at[c], {"seq": 2 - pair}
        )

    def own_copy(pair, c, clip):
        return same(att.at[clip, pl.ds(2 * pair, 2), :, cut(c)], own_send, own_recv.at[c], mate)

    def fwd_copy(pair, c, clip):
        return same(att.at[clip, pl.ds(2 * pair, 2), :, cut(c)], fwd_send, fwd_recv.at[c], mate)

    def back_copy(block, c, target):
        return remote(
            stage.at[:, block, :, cut(c)],
            back.at[:, block, :, cut(c)],
            back_send,
            back_recv.at[block, c],
            {"seq": target},
        )

    def res_copy(which, c):
        return remote(
            outs.at[which, :, cut(c)],
            (dq_ref, dk_ref, dv_ref)[which].at[:, cut(c)],
            res_send,
            res_recv.at[which, c],
            {"seq": 3},
        )

    def part_copy(c, target):
        return remote(part.at[:, cut(c)], landed.at[:, cut(c)], part_send, part_recv.at[c], {"seq": target})

    own_rows = pl.ds(pl.multiple_of(s * tok, tok), tok)
    loads = [
        pltpu.make_async_copy(k_hbm, kv.at[0, own_rows, :], load_sem.at[0]),
        pltpu.make_async_copy(v_hbm, kv.at[1, own_rows, :], load_sem.at[1]),
        pltpu.make_async_copy(og_hbm, og_ref, load_sem.at[2]),
        pltpu.make_async_copy(pattern_hbm, pattern_ref, load_sem.at[3]),
        pltpu.make_async_copy(q_hbm, q_ref.at[0], load_sem.at[4]),
        pltpu.make_async_copy(w_hbm, w_ref, load_sem.at[5]),
    ]

    barrier = pltpu.get_barrier_semaphore()
    for other in range(4):
        for mine in range(4):
            if mine != other and abs(mine - other) < 3:

                @pl.when(s == mine)
                def _(other=other):
                    pl.semaphore_signal(barrier, inc=1, device_id={"seq": other}, device_id_type=MESH)

    pl.semaphore_signal(barrier, inc=1, device_id=mate, device_id_type=MESH)
    pl.semaphore_signal(barrier, inc=1, device_id={"head": 1 - h}, device_id_type=MESH)
    for load in loads:
        load.start()
    loads[3].wait()
    line = lax.broadcasted_iota(jnp.int32, (8, 128), 0)
    info[s] = jnp.where(
        line == 0, valid_ref[0, 0], jnp.where(line == 1, pattern_ref[0, 0], pattern_ref[0, 1])
    )
    loads[0].wait()
    loads[1].wait()
    pl.semaphore_wait(barrier, 4 + lax.rem((s + 1) // 2, 2))

    @pl.when(s == 0)
    def _():
        for c in range(2):
            edge_kv(0, c).start()
        info_copy(0, 1, 0).start()
        info_copy(0, 2, 1).start()

    @pl.when(s == 1)
    def _():
        for c in range(2):
            kv_copy(1, c).start()
        info_copy(1, 2, 0).start()

    @pl.when(s == 3)
    def _():
        info_copy(3, 2, 0).start()
        edge_kv(3, 0).start()

    loads[2].wait()
    half_copy().start()

    @pl.when(s == 2)
    def _():
        for piece in (0, 1):
            og_copy(2, 0, piece).start()

    loads[4].wait()

    @pl.when(s == 3)
    def _():
        edge_q(0).start()
        og_copy(3, 0, 0).start()

    @pl.when(s == 0)
    def _():
        og_copy(0, 1, 0).start()
        og_copy(0, 0, 0).start()
        for c in (2, 3):
            edge_kv(0, c).start()

    lhs[0] = og_ref[:, pl.ds(pl.multiple_of(d * half, half), half)]
    loads[5].wait()
    half_copy().wait_recv()
    both = lhs[...].reshape(2 * tok, half)
    for c in range(width // GRAD_CHUNK):
        place = pl.ds(c * GRAD_CHUNK, GRAD_CHUNK)
        product = dot_nn(both, w_ref[:, place])
        gacc[:, place] = product[:tok]
        gsend[:, place] = product[tok:].astype(BF16)
        gx_copy(c).start()

    @pl.when(s == 1)
    def _():
        edge_kv(0, 0).wait_recv()
        kv_copy(0, 0).start()
        kv_copy(1, 2).start()
        edge_kv(0, 1).wait_recv()
        kv_copy(0, 1).start()
        og_copy(1, 1, 0).start()

    for block in (1, 2):

        @pl.when(s == block)
        def _(block=block):
            for piece in (0, 1):
                cols[d, piece, block] = og_ref[:, own_columns(block // 2, piece)]
                mate_copy(block, piece, d).start()

    for c in range(width // GRAD_CHUNK):
        place = pl.ds(c * GRAD_CHUNK, GRAD_CHUNK)
        gx_copy(c).wait_recv()
        g_ref[0, :, place] = (gacc[:, place] + grecv[:, place].astype(F32)).astype(BF16)

        @pl.when(s == 3)
        def _(c=c):
            for inner in (2 * c, 2 * c + 1):
                edge_g(inner).start()
            if c == 0:
                og_copy(3, 0, 1).start()
            if c == 1:
                og_copy(3, 1, 0).start()
            if c == 3:
                og_copy(3, 1, 1).start()
            for inner in (2 * c + 1, 2 * c + 2):
                if inner < heads:
                    edge_kv(3, inner).start()
                    edge_q(inner).start()

    lane = lax.broadcasted_iota(jnp.int32, (1, HEAD), 1)

    def shade(row_block, key_blocks):
        rows = []
        for key_block in key_blocks:
            seen = lane < info[key_block, 0:1, :]
            level = row_block - key_block
            if level:
                seen = jnp.logical_and(seen, info[row_block, level : level + 1, :] > 0)
            rows.append(jnp.where(seen, 0.0, masked_score))
        return jnp.concatenate(rows, axis=1)

    firsts = (0, wide - rows_out)

    def product(piece, place, count):
        return dot_tn(pick[piece].reshape(8 * tok, wide), att[:, :, :, place].reshape(8 * tok, count))

    def weigh_edge(role, c):
        own_copy(role - 1, c, 1 - d).wait_recv()
        fwd_copy(2 - role, c, 1 - d).wait_recv()
        full = product(0, cut(c), HEAD)
        for clip in (0, 1):

            @pl.when(d == clip)
            def _(clip=clip):
                part[:, cut(c)] = full[firsts[clip] : firsts[clip] + rows_out].astype(BF16)

        part_copy(c, 3 * (role - 1)).start()

    def weigh_own():
        for c in range(width // GRAD_CHUNK):
            place = pl.ds(c * GRAD_CHUNK, GRAD_CHUNK)
            full = product(1, place, GRAD_CHUNK)
            for clip in (0, 1):

                @pl.when(d == clip)
                def _(clip=clip):
                    wg_ref[:, place] = full[firsts[clip] : firsts[clip] + rows_out]

    def forward_rows(role, block, piece):
        og_copy(block, role - 1, piece).wait_recv()
        x_copy(block, piece, True).start()

    def forward_mate(role, block, piece):
        x_copy(block, piece, False).wait_recv()
        mate_copy(block, piece, d).start()

    def gather_columns(piece):
        for block in range(4):
            mate_copy(block, piece, 1 - d).wait_recv()
        first = pl.multiple_of(d * (seg - wide), HEAD)
        pick[piece] = cols[:, piece, :, :, pl.ds(first, wide)]

    @pl.when(s == 0)
    def _():
        bias = shade(0, (0,))
        for c in range(heads):
            hs = cut(c)
            attended, dq, dk, dv = attention(
                q_ref[0, :, hs], g_ref[0, :, hs], kv[0, :tok, hs], kv[1, :tok, hs], bias
            )
            att[d, 0, :, hs] = attended
            dq_ref[:, hs] = dq
            acc[0, 0, :, hs] = dk
            acc[1, 0, :, hs] = dv
            edge_att(c).start()
            if c + 4 < heads:
                edge_kv(0, c + 4).start()
            if c == 5:
                og_copy(0, 0, 1).start()
            if c == 7:
                og_copy(0, 1, 1).start()
        for c in range(heads):
            hs = cut(c)
            back_copy(0, c, 1).wait_recv()
            dk_ref[:, hs] = (acc[0, 0, :, hs] + back[0, 0, :, hs].astype(F32)).astype(BF16)
            dv_ref[:, hs] = (acc[1, 0, :, hs] + back[1, 0, :, hs].astype(F32)).astype(BF16)
            part_copy(c, 1).wait_recv()
            wg_ref[:, hs] = landed[:, hs].astype(F32)

    @pl.when(s == 1)
    def _():
        info_copy(0, 2, 0).wait_recv()
        bias = shade(1, (0, 1))
        for block in (2, 3, 0):
            forward_rows(1, block, 0)
        for c in range(heads + 2):
            if c < heads:
                hs = cut(c)
                attended, dq, dk, dv = attention(
                    q_ref[0, :, hs], g_ref[0, :, hs], kv[0, : 2 * tok, hs], kv[1, : 2 * tok, hs], bias
                )
                att[d, 1, :, hs] = attended
                dq_ref[:, hs] = dq
                for at, grad in ((0, dk), (1, dv)):
                    acc[at, 0, :, hs] = grad[:tok]
                    acc[at, 1, :, hs] = grad[tok:]
                if c + 2 < heads:
                    edge_kv(0, c + 2).wait_recv()
                    kv_copy(0 if c == 0 else 2, c + 2).start()
                edge_att(c).wait_recv()
                att_copy(0, c).start()
                own_copy(0, c, d).start()
                if c == 6:
                    og_copy(1, 1, 1).start()
            if c == 0:
                for block in (2, 3, 0):
                    forward_mate(1, block, 0)
            if c == 1:
                gather_columns(0)
                for block in (2, 3):
                    forward_rows(1, block, 1)
            if c == 2:
                for block in (2, 3):
                    forward_mate(1, block, 1)
            if c == 7:
                forward_rows(1, 0, 1)
            if c == 8:
                forward_mate(1, 0, 1)
            j = c - 2
            if 0 <= j < heads:
                hs = cut(j)
                att_copy(1, j).wait_recv()
                fwd_copy(1, j, d).start()
                back_copy(0, j, 1).wait_recv()
                stage[:, 0, :, hs] = (acc[:, 0, :, hs] + back[:, 0, :, hs].astype(F32)).astype(BF16)
                back_copy(0, j, 0).start()
                weigh_edge(1, j)
                back_copy(1, j, 1).wait_recv()
                total = acc[:, 1, :, hs] + back[:, 1, :, hs].astype(F32)
                dk_ref[:, hs] = total[0].astype(BF16)
                dv_ref[:, hs] = total[1].astype(BF16)
        gather_columns(1)
        weigh_own()

    @pl.when(s == 2)
    def _():
        for block in (0, 1, 3):
            info_copy(block, 2, 0).wait_recv()
        bias_own = shade(2, (0, 1, 2))
        bias_edge = shade(3, (1, 2, 3))
        for c in range(heads + 2):
            if c < heads:
                hs = cut(c)
                if c < 3:
                    kv_copy(1, c).wait_recv()
                    kv_copy(0, c).wait_recv()
                else:
                    kv_copy(2, c).wait_recv()
                edge_kv(3, c).wait_recv()
                edge_q(c).wait_recv()
                edge_g(c).wait_recv()
                own = attention(
                    q_ref[0, :, hs], g_ref[0, :, hs], kv[0, : 3 * tok, hs], kv[1, : 3 * tok, hs], bias_own
                )
                edge = attention(
                    q_ref[1, :, hs], g_ref[1, :, hs], kv[0, tok:, hs], kv[1, tok:, hs], bias_edge
                )
                att[d, 2, :, hs] = own[0]
                att[d, 3, :, hs] = edge[0]
                att_copy(1, c).start()
                for at in (0, 1):
                    stage[at, 0, :, hs] = own[2 + at][:tok].astype(BF16)
                    stage[at, 1, :, hs] = (own[2 + at][tok : 2 * tok] + edge[2 + at][:tok]).astype(BF16)
                back_copy(0, c, 1).start()
                back_copy(1, c, 1).start()
                own_copy(1, c, d).start()
                outs[0, :, hs] = edge[1]
                for at in (0, 1):
                    outs[1 + at, :, hs] = edge[2 + at][2 * tok :].astype(BF16)
                for which in range(3):
                    res_copy(which, c).start()
                dq_ref[:, hs] = own[1]
                dk_ref[:, hs] = (own[2][2 * tok :] + edge[2][tok : 2 * tok]).astype(BF16)
                dv_ref[:, hs] = (own[3][2 * tok :] + edge[3][tok : 2 * tok]).astype(BF16)
            if c == 1:
                for block in (0, 1, 3):
                    forward_rows(2, block, 0)
                for block in (0, 1, 3):
                    forward_mate(2, block, 0)
            if c == 2:
                gather_columns(0)
            j = c - 2
            if 0 <= j < heads:
                att_copy(0, j).wait_recv()
                fwd_copy(0, j, d).start()
                weigh_edge(2, j)
            if c == heads - 1:
                for block in (0, 1, 3):
                    forward_rows(2, block, 1)
            if c == heads:
                for block in (0, 1, 3):
                    forward_mate(2, block, 1)
        gather_columns(1)
        weigh_own()

    @pl.when(s == 3)
    def _():
        for c in range(heads):
            for which in range(3):
                res_copy(which, c).wait_recv()
            part_copy(c, 3).wait_recv()
            wg_ref[:, cut(c)] = landed[:, cut(c)].astype(F32)

    def all_sent(place, send):
        remote(place, place, send, half_recv, mate).wait_send()

    half_copy().wait_send()
    all_sent(gsend, gx_send)
    half_og = og_ref.at[half_rows(0), pl.ds(0, 2 * seg)]

    @pl.when(s == 0)
    def _():
        for target in (1, 2):
            info_copy(0, target, target - 1).wait_send()
        all_sent(kv.at[:, pl.ds(0, tok), :], edge_send.at[0])
        all_sent(att.at[d, 0], edge_send.at[1])
        all_sent(half_og, near_send)
        all_sent(half_og, far_send)

    @pl.when(s == 3)
    def _():
        info_copy(3, 2, 0).wait_send()
        all_sent(kv.at[:, pl.ds(3 * tok, tok), :], edge_send.at[0])
        all_sent(q_ref.at[0], edge_send.at[1])
        all_sent(g_ref.at[0], edge_send.at[2])
        all_sent(half_og, near_send)
        all_sent(half_og, far_send)

    for role in (1, 2):

        @pl.when(s == role)
        def _(role=role):
            all_sent(half_og, far_send)
            all_sent(cols.at[d, :, pl.ds(0, 3), half_rows(0), :], x_send)
            all_sent(cols.at[d], mate_send)
            pair = att.at[d, pl.ds(2 * (role - 1), 2)]
            all_sent(pair, att_send)
            all_sent(pair, own_send)
            all_sent(pair, fwd_send)
            all_sent(part, part_send)
            if role == 1:
                info_copy(1, 2, 0).wait_send()
                all_sent(kv.at[:, pl.ds(0, 2 * tok), :], kv_send)
                all_sent(stage.at[:, 0], back_send)
            else:
                all_sent(stage, back_send)
                all_sent(outs, res_send)


def out_kernel(*refs):
    count = len(refs) // 2
    sems = refs[-1]
    copies = [pltpu.make_async_copy(refs[i], refs[count + i], sems.at[i]) for i in range(count)]
    for copy in copies:
        copy.start()
    for copy in copies:
        copy.wait()


def write_out(arrays):
    return pl.pallas_call(
        out_kernel,
        out_shape=tuple(jax.ShapeDtypeStruct(a.shape, a.dtype) for a in arrays),
        in_specs=[pl.BlockSpec(memory_space=pltpu.VMEM)] * len(arrays),
        out_specs=(pl.BlockSpec(memory_space=pltpu.HBM),) * len(arrays),
        scratch_shapes=[pltpu.SemaphoreType.DMA((len(arrays),))],
        compiler_params=pltpu.CompilerParams(vmem_limit_bytes=4 * 1024 * 1024),
    )(*arrays)


def fused(queries, keys, values, out_grad, out_weight, pattern, valid):
    _, tok, width = queries.shape
    columns = out_grad.shape[2]
    rows_out = columns // 8
    half = out_weight.shape[0]
    heads = width // HEAD
    chunks = width // GRAD_CHUNK
    wide = -(-rows_out // HEAD) * HEAD
    vmem = pl.BlockSpec(memory_space=pltpu.VMEM)
    hbm = pl.BlockSpec(memory_space=pltpu.HBM)
    smem = pl.BlockSpec(memory_space=pltpu.SMEM)
    dma = pltpu.SemaphoreType.DMA
    rows_bf = jax.ShapeDtypeStruct((tok, width), BF16)
    inputs = (pattern, queries[0], keys[0], values[0], out_grad[0], out_weight)
    outs = pl.pallas_call(
        functools.partial(kernel, rows_out),
        out_shape=(rows_bf, rows_bf, rows_bf, jax.ShapeDtypeStruct((rows_out, width), F32)),
        in_specs=[smem] + [hbm] * 6,
        out_specs=(vmem,) * 4,
        scratch_shapes=[
            pltpu.VMEM((2, tok, width), BF16),
            pltpu.VMEM((tok, columns), BF16),
            pltpu.VMEM((half, width), BF16),
            pltpu.VMEM((2, 4 * tok, width), BF16),
            pltpu.VMEM((4, 8, 128), jnp.int32),
            pltpu.VMEM((2, tok, half), BF16),
            pltpu.VMEM((tok, width), F32),
            pltpu.VMEM((tok, width), BF16),
            pltpu.VMEM((tok, width), BF16),
            pltpu.VMEM((2, tok, width), BF16),
            pltpu.VMEM((2, 2, tok, width), F32),
            pltpu.VMEM((2, 2, tok, width), BF16),
            pltpu.VMEM((2, 2, tok, width), BF16),
            pltpu.VMEM((3, tok, width), BF16),
            pltpu.VMEM((2, 4, tok, width), BF16),
            pltpu.VMEM((2, 2, 4, tok, columns // 4), BF16),
            pltpu.VMEM((2, 2, 4, tok, wide), BF16),
            pltpu.VMEM((rows_out, width), BF16),
            pltpu.VMEM((rows_out, width), BF16),
            pltpu.SMEM((1, 2), jnp.int32),
            dma((6,)),
            dma((2,)),
            dma((4,)),
            dma,
            dma,
            dma,
            dma((chunks,)),
            dma,
            dma((2, heads)),
            dma((3,)),
            dma((3, heads)),
            dma,
            dma,
            dma((4, 2)),
            dma,
            dma((4, 2)),
            dma,
            dma((4, 2)),
            dma,
            dma((heads,)),
            dma,
            dma((heads,)),
            dma,
            dma((heads,)),
            dma,
            dma((2, heads)),
            dma,
            dma((3, heads)),
            dma,
            dma((heads,)),
        ],
        compiler_params=pltpu.CompilerParams(
            collective_id=0, has_side_effects=True, vmem_limit_bytes=48 * 1024 * 1024
        ),
    )(valid, *[pltpu.with_memory_space_constraint(a, pltpu.HBM) for a in inputs])
    outs = write_out(outs)
    return outs[0][None], outs[1][None], outs[2][None], outs[3]


def solution(mesh):
    body = local
    if mesh.shape["seq"] == 4 and mesh.shape["dp"] == 2 and mesh.shape["head"] == 2:
        body = fused
    return jax.shard_map(
        body,
        mesh=mesh,
        in_specs=(
            P(("groups", "dp"), "seq", "head"),
            P(("groups", "dp"), "seq", "head"),
            P(("groups", "dp"), "seq", "head"),
            P(("groups", "dp"), "seq", None),
            P("dp", "head"),
            P("seq", None),
            P(("groups", "dp"), "seq"),
        ),
        out_specs=(
            P(("groups", "dp"), "seq", "head"),
            P(("groups", "dp"), "seq", "head"),
            P(("groups", "dp"), "seq", "head"),
            P(("groups", "seq", "dp"), "head"),
        ),
        check_vma=False,
    )
```

```python
import functools

import jax
import jax.numpy as jnp
from jax import lax
from jax.experimental import pallas as pl
from jax.experimental.pallas import tpu as pltpu
from jax.sharding import PartitionSpec as P

HEAD = 128


head_scale = 0.08838834764831845
masked_score = -1e30


def from_behind(value, axis, steps):
    count = lax.axis_size(axis)
    first, last = (max(0, -steps), min(count, count - steps))
    return lax.ppermute(value, axis, [(source, source + steps) for source in range(first, last)])


def split_heads(matrix):
    return matrix.reshape(matrix.shape[0], matrix.shape[1], -1, HEAD)


def local(queries, keys, values, out_grad, out_weight, pattern, valid):
    clip_count, row_count, width_dev = queries.shape
    levels = lax.axis_size("seq").bit_length() - 1
    positions = jnp.arange(row_count, dtype=jnp.int32)
    key_list = [keys]
    value_list = [values]
    visible_list = [positions[None, :] < valid]
    for level_index in range(levels):
        far_keys, far_values, far_valid = from_behind((keys, values, valid), "seq", 2**level_index)
        key_list.append(far_keys)
        value_list.append(far_values)
        visible_list.append((positions[None, :] < far_valid) & (pattern[0, level_index] > 0))
    key_heads = split_heads(jnp.concatenate(key_list, axis=1))
    value_heads = split_heads(jnp.concatenate(value_list, axis=1))
    visible = jnp.concatenate(visible_list, axis=1)
    query_heads = split_heads(queries)
    scores = (
        jnp.einsum("cqhd,ckhd->chqk", query_heads, key_heads, preferred_element_type=jnp.float32)
        * head_scale
    )
    scores = jnp.where(visible[:, None, None, :], scores, masked_score)
    row_max = jnp.max(scores, axis=-1, keepdims=True)
    log_total = row_max + jnp.log(jnp.sum(jnp.exp(scores - row_max), axis=-1, keepdims=True))
    probs_full = jnp.exp(scores - log_total)
    weights = probs_full.astype(jnp.bfloat16)
    attended = jnp.einsum(
        "chqk,ckhd->cqhd", weights, value_heads, preferred_element_type=jnp.float32
    ).astype(jnp.bfloat16)
    columns = out_grad
    grad_in = jnp.einsum(
        "cqe,eh->cqh",
        columns,
        lax.all_gather(out_weight, "dp", axis=0, tiled=True),
        preferred_element_type=jnp.float32,
    ).astype(jnp.bfloat16)
    grad_heads = split_heads(grad_in)
    row_delta = jnp.einsum(
        "cqhd,cqhd->chq", grad_heads.astype(jnp.float32), attended.astype(jnp.float32)
    )
    value_grad_all = jnp.einsum(
        "chqk,cqhd->ckhd", weights, grad_heads, preferred_element_type=jnp.float32
    )
    prob_grad = jnp.einsum(
        "cqhd,ckhd->chqk", grad_heads, value_heads, preferred_element_type=jnp.float32
    )
    score_grad = (probs_full * (prob_grad - row_delta[..., None])).astype(jnp.bfloat16)
    query_grad = (
        jnp.einsum("chqk,ckhd->cqhd", score_grad, key_heads, preferred_element_type=jnp.float32)
        * head_scale
    )
    key_grad_all = (
        jnp.einsum("chqk,cqhd->ckhd", score_grad, query_heads, preferred_element_type=jnp.float32)
        * head_scale
    )
    key_grad_all = key_grad_all.reshape(clip_count, -1, width_dev)
    value_grad_all = value_grad_all.reshape(clip_count, -1, width_dev)
    key_parts = [
        key_grad_all[:, set_index * row_count : (set_index + 1) * row_count]
        for set_index in range(levels + 1)
    ]
    value_parts = [
        value_grad_all[:, set_index * row_count : (set_index + 1) * row_count]
        for set_index in range(levels + 1)
    ]
    key_total = key_parts[0]
    value_total = value_parts[0]
    for level_index in range(levels):
        back_keys, back_values = (
            from_behind(
                key_parts[level_index + 1].astype(jnp.bfloat16), "seq", -(2**level_index)
            ).astype(jnp.float32),
            from_behind(
                value_parts[level_index + 1].astype(jnp.bfloat16), "seq", -(2**level_index)
            ).astype(jnp.float32),
        )
        key_total = key_total + back_keys
        value_total = value_total + back_values
    attended_rows = attended.reshape(clip_count, row_count, width_dev)
    columns = out_grad
    seq_total = lax.psum_scatter(
        jnp.einsum(
            "cqe,cqh->eh", columns, attended_rows, preferred_element_type=jnp.float32
        ).astype(jnp.bfloat16),
        "seq",
        scatter_dimension=0,
        tiled=True,
    )
    weight_grad = lax.psum_scatter(seq_total, "dp", scatter_dimension=0, tiled=True).astype(
        jnp.float32
    )
    query_out = query_grad.astype(jnp.bfloat16).reshape(clip_count, row_count, width_dev)
    return (
        query_out,
        key_total.astype(jnp.bfloat16),
        value_total.astype(jnp.bfloat16),
        weight_grad,
    )


MESH = pl.DeviceIdType.MESH
F32 = jnp.float32
BF16 = jnp.bfloat16
GRAD_CHUNK = 2 * HEAD


def dot_nn(a, b):
    return lax.dot_general(a, b, (((1,), (0,)), ((), ())), preferred_element_type=F32)


def dot_nt(a, b):
    return lax.dot_general(a, b, (((1,), (1,)), ((), ())), preferred_element_type=F32)


def dot_tn(a, b):
    return lax.dot_general(a, b, (((0,), (0,)), ((), ())), preferred_element_type=F32)


def attention(q, g, k, v, bias):
    scores = dot_nt(q, k) * head_scale + bias
    top = jnp.max(scores, axis=1, keepdims=True)
    raised = jnp.exp(scores - top)
    probs = raised * (1.0 / jnp.sum(raised, axis=1, keepdims=True))
    weights = probs.astype(BF16)
    attended = dot_nn(weights, v).astype(BF16)
    delta = jnp.sum(g.astype(F32) * attended.astype(F32), axis=1, keepdims=True)
    score_grad = (probs * (dot_nt(g, v) - delta)).astype(BF16)
    dq = (dot_nn(score_grad, k) * head_scale).astype(BF16)
    return attended, dq, dot_tn(score_grad, q) * head_scale, dot_tn(weights, g)


def kernel(
    rows_out,
    valid_ref,
    pattern_hbm,
    q_hbm,
    k_hbm,
    v_hbm,
    og_hbm,
    w_hbm,
    dq_ref,
    dk_ref,
    dv_ref,
    wg_ref,
    q_ref,
    og_ref,
    w_ref,
    kv,
    info,
    lhs,
    gacc,
    gsend,
    grecv,
    g_ref,
    acc,
    stage,
    back,
    outs,
    att,
    cols,
    pick,
    part,
    landed,
    pattern_ref,
    load_sem,
    info_send,
    info_recv,
    half_send,
    half_recv,
    gx_send,
    gx_recv,
    kv_send,
    kv_recv,
    edge_send,
    edge_recv,
    near_send,
    far_send,
    og_recv,
    x_send,
    x_recv,
    mate_send,
    mate_recv,
    att_send,
    att_recv,
    own_send,
    own_recv,
    fwd_send,
    fwd_recv,
    back_send,
    back_recv,
    res_send,
    res_recv,
    part_send,
    part_recv,
):
    s = lax.axis_index("seq")
    d = lax.axis_index("dp")
    h = lax.axis_index("head")
    tok, width = dq_ref.shape
    half = w_ref.shape[0]
    heads = width // HEAD
    seg = cols.shape[4]
    wide = pick.shape[4]
    mate = {"dp": 1 - d}
    part_rows = tok // 2

    def remote(src, dst, send, recv, device):
        return pltpu.make_async_remote_copy(
            src_ref=src, dst_ref=dst, send_sem=send, recv_sem=recv, device_id=device, device_id_type=MESH
        )

    def same(place, send, recv, device):
        return remote(place, place, send, recv, device)

    def cut(c):
        return pl.ds(c * HEAD, HEAD)

    def info_copy(block, target, slot):
        return same(info.at[block], info_send.at[slot], info_recv.at[block], {"seq": target})

    def half_copy():
        other = pl.multiple_of((1 - d) * half, half)
        return remote(og_ref.at[:, pl.ds(other, half)], lhs.at[1], half_send, half_recv, mate)

    def gx_copy(c):
        place = pl.ds(c * GRAD_CHUNK, GRAD_CHUNK)
        return remote(gsend.at[:, place], grecv.at[:, place], gx_send, gx_recv.at[c], mate)

    def kv_copy(which, c):
        first, count = ((0, 1), (1, 1), (0, 2))[which]
        place = kv.at[:, pl.ds(first * tok, count * tok), cut(c)]
        slot = 1 if which == 1 else 0
        return same(place, kv_send, kv_recv.at[slot, c], {"seq": 2})

    def edge_kv(block, c):
        place = kv.at[:, pl.ds(block * tok, tok), cut(c)]
        return same(place, edge_send.at[0], edge_recv.at[0, c], {"seq": 1 + block // 2})

    def edge_q(c):
        return remote(
            q_ref.at[0, :, cut(c)], q_ref.at[1, :, cut(c)], edge_send.at[1], edge_recv.at[1, c], {"seq": 2}
        )

    def edge_g(c):
        return remote(
            g_ref.at[0, :, cut(c)], g_ref.at[1, :, cut(c)], edge_send.at[2], edge_recv.at[2, c], {"seq": 2}
        )

    def edge_att(c):
        return same(att.at[d, 0, :, cut(c)], edge_send.at[1], edge_recv.at[1, c], {"seq": 1})

    def half_rows(row):
        return pl.ds(pl.multiple_of(row * part_rows, part_rows), part_rows)

    def own_columns(side, piece):
        return pl.ds((2 * side + (piece if side == 0 else 1 - piece)) * seg, seg)

    def og_copy(block, side, piece):
        sems = near_send if block // 2 == side else far_send
        return remote(
            og_ref.at[half_rows(h), own_columns(side, piece)],
            cols.at[d, piece, block, half_rows(h), :],
            sems,
            og_recv.at[block, piece],
            {"seq": 1 + side},
        )

    def x_copy(block, piece, mine):
        place = cols.at[d, piece, block, half_rows(h if mine else 1 - h), :]
        return same(place, x_send, x_recv.at[block, piece], {"head": 1 - h})

    def mate_copy(block, piece, clip):
        return same(cols.at[clip, piece, block], mate_send, mate_recv.at[block, piece], mate)

    def att_copy(pair, c):
        return same(
            att.at[d, pl.ds(2 * pair, 2), :, cut(c)], att_send, att_recv.at[c], {"seq": 2 - pair}
        )

    def own_copy(pair, c, clip):
        return same(att.at[clip, pl.ds(2 * pair, 2), :, cut(c)], own_send, own_recv.at[c], mate)

    def fwd_copy(pair, c, clip):
        return same(att.at[clip, pl.ds(2 * pair, 2), :, cut(c)], fwd_send, fwd_recv.at[c], mate)

    def back_copy(block, c, target):
        return remote(
            stage.at[:, block, :, cut(c)],
            back.at[:, block, :, cut(c)],
            back_send,
            back_recv.at[block, c],
            {"seq": target},
        )

    def res_copy(which, c):
        return remote(
            outs.at[which, :, cut(c)],
            (dq_ref, dk_ref, dv_ref)[which].at[:, cut(c)],
            res_send,
            res_recv.at[which, c],
            {"seq": 3},
        )

    def part_copy(c, target):
        return remote(part.at[:, cut(c)], landed.at[:, cut(c)], part_send, part_recv.at[c], {"seq": target})

    own_rows = pl.ds(pl.multiple_of(s * tok, tok), tok)
    loads = [
        pltpu.make_async_copy(k_hbm, kv.at[0, own_rows, :], load_sem.at[0]),
        pltpu.make_async_copy(v_hbm, kv.at[1, own_rows, :], load_sem.at[1]),
        pltpu.make_async_copy(og_hbm, og_ref, load_sem.at[2]),
        pltpu.make_async_copy(pattern_hbm, pattern_ref, load_sem.at[3]),
        pltpu.make_async_copy(q_hbm, q_ref.at[0], load_sem.at[4]),
        pltpu.make_async_copy(w_hbm, w_ref, load_sem.at[5]),
    ]

    barrier = pltpu.get_barrier_semaphore()
    for other in range(4):
        for mine in range(4):
            if mine != other and abs(mine - other) < 3:

                @pl.when(s == mine)
                def _(other=other):
                    pl.semaphore_signal(barrier, inc=1, device_id={"seq": other}, device_id_type=MESH)

    pl.semaphore_signal(barrier, inc=1, device_id=mate, device_id_type=MESH)
    pl.semaphore_signal(barrier, inc=1, device_id={"head": 1 - h}, device_id_type=MESH)
    for load in loads:
        load.start()
    loads[3].wait()
    line = lax.broadcasted_iota(jnp.int32, (8, 128), 0)
    info[s] = jnp.where(
        line == 0, valid_ref[0, 0], jnp.where(line == 1, pattern_ref[0, 0], pattern_ref[0, 1])
    )
    loads[0].wait()
    loads[1].wait()
    pl.semaphore_wait(barrier, 4 + lax.rem((s + 1) // 2, 2))

    @pl.when(s == 0)
    def _():
        for c in range(2):
            edge_kv(0, c).start()
        info_copy(0, 1, 0).start()
        info_copy(0, 2, 1).start()

    @pl.when(s == 1)
    def _():
        for c in range(2):
            kv_copy(1, c).start()
        info_copy(1, 2, 0).start()

    @pl.when(s == 3)
    def _():
        info_copy(3, 2, 0).start()
        edge_kv(3, 0).start()

    loads[2].wait()
    half_copy().start()

    @pl.when(s == 2)
    def _():
        for piece in (0, 1):
            og_copy(2, 0, piece).start()

    loads[4].wait()

    @pl.when(s == 3)
    def _():
        edge_q(0).start()
        og_copy(3, 0, 0).start()

    @pl.when(s == 0)
    def _():
        og_copy(0, 1, 0).start()
        og_copy(0, 0, 0).start()
        for c in (2, 3):
            edge_kv(0, c).start()

    lhs[0] = og_ref[:, pl.ds(pl.multiple_of(d * half, half), half)]
    loads[5].wait()
    half_copy().wait_recv()
    both = lhs[...].reshape(2 * tok, half)
    for c in range(width // GRAD_CHUNK):
        place = pl.ds(c * GRAD_CHUNK, GRAD_CHUNK)
        product = dot_nn(both, w_ref[:, place])
        gacc[:, place] = product[:tok]
        gsend[:, place] = product[tok:].astype(BF16)
        gx_copy(c).start()

    @pl.when(s == 1)
    def _():
        edge_kv(0, 0).wait_recv()
        kv_copy(0, 0).start()
        kv_copy(1, 2).start()
        edge_kv(0, 1).wait_recv()
        kv_copy(0, 1).start()
        og_copy(1, 1, 0).start()

    for block in (1, 2):

        @pl.when(s == block)
        def _(block=block):
            for piece in (0, 1):
                cols[d, piece, block] = og_ref[:, own_columns(block // 2, piece)]
                mate_copy(block, piece, d).start()

    for c in range(width // GRAD_CHUNK):
        place = pl.ds(c * GRAD_CHUNK, GRAD_CHUNK)
        gx_copy(c).wait_recv()
        g_ref[0, :, place] = (gacc[:, place] + grecv[:, place].astype(F32)).astype(BF16)

        @pl.when(s == 3)
        def _(c=c):
            for inner in (2 * c, 2 * c + 1):
                edge_g(inner).start()
            if c == 0:
                og_copy(3, 0, 1).start()
            if c == 1:
                og_copy(3, 1, 0).start()
            if c == 3:
                og_copy(3, 1, 1).start()
            for inner in (2 * c + 1, 2 * c + 2):
                if inner < heads:
                    edge_kv(3, inner).start()
                    edge_q(inner).start()

    lane = lax.broadcasted_iota(jnp.int32, (1, HEAD), 1)

    def shade(row_block, key_blocks):
        rows = []
        for key_block in key_blocks:
            seen = lane < info[key_block, 0:1, :]
            level = row_block - key_block
            if level:
                seen = jnp.logical_and(seen, info[row_block, level : level + 1, :] > 0)
            rows.append(jnp.where(seen, 0.0, masked_score))
        return jnp.concatenate(rows, axis=1)

    firsts = (0, wide - rows_out)

    def product(piece, place, count):
        return dot_tn(pick[piece].reshape(8 * tok, wide), att[:, :, :, place].reshape(8 * tok, count))

    def weigh_edge(role, c):
        own_copy(role - 1, c, 1 - d).wait_recv()
        fwd_copy(2 - role, c, 1 - d).wait_recv()
        full = product(0, cut(c), HEAD)
        for clip in (0, 1):

            @pl.when(d == clip)
            def _(clip=clip):
                part[:, cut(c)] = full[firsts[clip] : firsts[clip] + rows_out].astype(BF16)

        part_copy(c, 3 * (role - 1)).start()

    def weigh_own():
        for c in range(width // GRAD_CHUNK):
            place = pl.ds(c * GRAD_CHUNK, GRAD_CHUNK)
            full = product(1, place, GRAD_CHUNK)
            for clip in (0, 1):

                @pl.when(d == clip)
                def _(clip=clip):
                    wg_ref[:, place] = full[firsts[clip] : firsts[clip] + rows_out]

    def forward_rows(role, block, piece):
        og_copy(block, role - 1, piece).wait_recv()
        x_copy(block, piece, True).start()

    def forward_mate(role, block, piece):
        x_copy(block, piece, False).wait_recv()
        mate_copy(block, piece, d).start()

    def gather_columns(piece):
        for block in range(4):
            mate_copy(block, piece, 1 - d).wait_recv()
        first = pl.multiple_of(d * (seg - wide), HEAD)
        pick[piece] = cols[:, piece, :, :, pl.ds(first, wide)]

    @pl.when(s == 0)
    def _():
        bias = shade(0, (0,))
        for c in range(heads):
            hs = cut(c)
            attended, dq, dk, dv = attention(
                q_ref[0, :, hs], g_ref[0, :, hs], kv[0, :tok, hs], kv[1, :tok, hs], bias
            )
            att[d, 0, :, hs] = attended
            dq_ref[:, hs] = dq
            acc[0, 0, :, hs] = dk
            acc[1, 0, :, hs] = dv
            edge_att(c).start()
            if c + 4 < heads:
                edge_kv(0, c + 4).start()
            if c == 5:
                og_copy(0, 0, 1).start()
            if c == 7:
                og_copy(0, 1, 1).start()
        for c in range(heads):
            hs = cut(c)
            back_copy(0, c, 1).wait_recv()
            dk_ref[:, hs] = (acc[0, 0, :, hs] + back[0, 0, :, hs].astype(F32)).astype(BF16)
            dv_ref[:, hs] = (acc[1, 0, :, hs] + back[1, 0, :, hs].astype(F32)).astype(BF16)
            part_copy(c, 1).wait_recv()
            wg_ref[:, hs] = landed[:, hs].astype(F32)

    @pl.when(s == 1)
    def _():
        info_copy(0, 2, 0).wait_recv()
        bias = shade(1, (0, 1))
        for block in (2, 3, 0):
            forward_rows(1, block, 0)
        for c in range(heads + 2):
            if c < heads:
                hs = cut(c)
                attended, dq, dk, dv = attention(
                    q_ref[0, :, hs], g_ref[0, :, hs], kv[0, : 2 * tok, hs], kv[1, : 2 * tok, hs], bias
                )
                att[d, 1, :, hs] = attended
                dq_ref[:, hs] = dq
                for at, grad in ((0, dk), (1, dv)):
                    acc[at, 0, :, hs] = grad[:tok]
                    acc[at, 1, :, hs] = grad[tok:]
                if c + 2 < heads:
                    edge_kv(0, c + 2).wait_recv()
                    kv_copy(0 if c == 0 else 2, c + 2).start()
                edge_att(c).wait_recv()
                att_copy(0, c).start()
                own_copy(0, c, d).start()
                if c == 6:
                    og_copy(1, 1, 1).start()
            if c == 0:
                for block in (2, 3, 0):
                    forward_mate(1, block, 0)
            if c == 1:
                gather_columns(0)
                for block in (2, 3):
                    forward_rows(1, block, 1)
            if c == 2:
                for block in (2, 3):
                    forward_mate(1, block, 1)
            if c == 7:
                forward_rows(1, 0, 1)
            if c == 8:
                forward_mate(1, 0, 1)
            j = c - 2
            if 0 <= j < heads:
                hs = cut(j)
                att_copy(1, j).wait_recv()
                fwd_copy(1, j, d).start()
                back_copy(0, j, 1).wait_recv()
                stage[:, 0, :, hs] = (acc[:, 0, :, hs] + back[:, 0, :, hs].astype(F32)).astype(BF16)
                back_copy(0, j, 0).start()
                weigh_edge(1, j)
                back_copy(1, j, 1).wait_recv()
                total = acc[:, 1, :, hs] + back[:, 1, :, hs].astype(F32)
                dk_ref[:, hs] = total[0].astype(BF16)
                dv_ref[:, hs] = total[1].astype(BF16)
        gather_columns(1)
        weigh_own()

    @pl.when(s == 2)
    def _():
        for block in (0, 1, 3):
            info_copy(block, 2, 0).wait_recv()
        bias_own = shade(2, (0, 1, 2))
        bias_edge = shade(3, (1, 2, 3))
        for c in range(heads + 3):
            if c < heads:
                hs = cut(c)
                if c < 3:
                    kv_copy(1, c).wait_recv()
                    kv_copy(0, c).wait_recv()
                else:
                    kv_copy(2, c).wait_recv()
                edge_kv(3, c).wait_recv()
                edge_q(c).wait_recv()
                edge_g(c).wait_recv()
                own = attention(
                    q_ref[0, :, hs], g_ref[0, :, hs], kv[0, : 3 * tok, hs], kv[1, : 3 * tok, hs], bias_own
                )
                edge = attention(
                    q_ref[1, :, hs], g_ref[1, :, hs], kv[0, tok:, hs], kv[1, tok:, hs], bias_edge
                )
                att[d, 2, :, hs] = own[0]
                att[d, 3, :, hs] = edge[0]
                att_copy(1, c).start()
                for at in (0, 1):
                    stage[at, 0, :, hs] = own[2 + at][:tok].astype(BF16)
                    stage[at, 1, :, hs] = (own[2 + at][tok : 2 * tok] + edge[2 + at][:tok]).astype(BF16)
                back_copy(0, c, 1).start()
                back_copy(1, c, 1).start()
                own_copy(1, c, d).start()
                outs[0, :, hs] = edge[1]
                for at in (0, 1):
                    outs[1 + at, :, hs] = edge[2 + at][2 * tok :].astype(BF16)
                for which in range(3):
                    res_copy(which, c).start()
                dq_ref[:, hs] = own[1]
                dk_ref[:, hs] = (own[2][2 * tok :] + edge[2][tok : 2 * tok]).astype(BF16)
                dv_ref[:, hs] = (own[3][2 * tok :] + edge[3][tok : 2 * tok]).astype(BF16)
            if c == 1:
                for block in (3, 0, 1):
                    forward_rows(2, block, 0)
            if c == 2:
                for block in (3, 0, 1):
                    forward_mate(2, block, 0)
            if c == 3:
                gather_columns(0)
            j = c - 2
            if 0 <= j < heads:
                att_copy(0, j).wait_recv()
                fwd_copy(0, j, d).start()
            if 0 <= c - 3 < heads:
                weigh_edge(2, c - 3)
            if c == heads - 1:
                for block in (0, 1, 3):
                    forward_rows(2, block, 1)
            if c == heads:
                for block in (0, 1, 3):
                    forward_mate(2, block, 1)
        gather_columns(1)
        weigh_own()

    @pl.when(s == 3)
    def _():
        for c in range(heads):
            for which in range(3):
                res_copy(which, c).wait_recv()
            part_copy(c, 3).wait_recv()
            wg_ref[:, cut(c)] = landed[:, cut(c)].astype(F32)

    def all_sent(place, send):
        remote(place, place, send, half_recv, mate).wait_send()

    half_copy().wait_send()
    all_sent(gsend, gx_send)
    half_og = og_ref.at[half_rows(0), pl.ds(0, 2 * seg)]

    @pl.when(s == 0)
    def _():
        for target in (1, 2):
            info_copy(0, target, target - 1).wait_send()
        all_sent(kv.at[:, pl.ds(0, tok), :], edge_send.at[0])
        all_sent(att.at[d, 0], edge_send.at[1])
        all_sent(half_og, near_send)
        all_sent(half_og, far_send)

    @pl.when(s == 3)
    def _():
        info_copy(3, 2, 0).wait_send()
        all_sent(kv.at[:, pl.ds(3 * tok, tok), :], edge_send.at[0])
        all_sent(q_ref.at[0], edge_send.at[1])
        all_sent(g_ref.at[0], edge_send.at[2])
        all_sent(half_og, near_send)
        all_sent(half_og, far_send)

    for role in (1, 2):

        @pl.when(s == role)
        def _(role=role):
            all_sent(half_og, far_send)
            all_sent(cols.at[d, :, pl.ds(0, 3), half_rows(0), :], x_send)
            all_sent(cols.at[d], mate_send)
            pair = att.at[d, pl.ds(2 * (role - 1), 2)]
            all_sent(pair, att_send)
            all_sent(pair, own_send)
            all_sent(pair, fwd_send)
            all_sent(part, part_send)
            if role == 1:
                info_copy(1, 2, 0).wait_send()
                all_sent(kv.at[:, pl.ds(0, 2 * tok), :], kv_send)
                all_sent(stage.at[:, 0], back_send)
            else:
                all_sent(stage, back_send)
                all_sent(outs, res_send)


def out_kernel(*refs):
    count = len(refs) // 2
    sems = refs[-1]
    copies = [pltpu.make_async_copy(refs[i], refs[count + i], sems.at[i]) for i in range(count)]
    for copy in copies:
        copy.start()
    for copy in copies:
        copy.wait()


def write_out(arrays):
    return pl.pallas_call(
        out_kernel,
        out_shape=tuple(jax.ShapeDtypeStruct(a.shape, a.dtype) for a in arrays),
        in_specs=[pl.BlockSpec(memory_space=pltpu.VMEM)] * len(arrays),
        out_specs=(pl.BlockSpec(memory_space=pltpu.HBM),) * len(arrays),
        scratch_shapes=[pltpu.SemaphoreType.DMA((len(arrays),))],
        compiler_params=pltpu.CompilerParams(vmem_limit_bytes=4 * 1024 * 1024),
    )(*arrays)


def fused(queries, keys, values, out_grad, out_weight, pattern, valid):
    _, tok, width = queries.shape
    columns = out_grad.shape[2]
    rows_out = columns // 8
    half = out_weight.shape[0]
    heads = width // HEAD
    chunks = width // GRAD_CHUNK
    wide = -(-rows_out // HEAD) * HEAD
    vmem = pl.BlockSpec(memory_space=pltpu.VMEM)
    hbm = pl.BlockSpec(memory_space=pltpu.HBM)
    smem = pl.BlockSpec(memory_space=pltpu.SMEM)
    dma = pltpu.SemaphoreType.DMA
    rows_bf = jax.ShapeDtypeStruct((tok, width), BF16)
    inputs = (pattern, queries[0], keys[0], values[0], out_grad[0], out_weight)
    outs = pl.pallas_call(
        functools.partial(kernel, rows_out),
        out_shape=(rows_bf, rows_bf, rows_bf, jax.ShapeDtypeStruct((rows_out, width), F32)),
        in_specs=[smem] + [hbm] * 6,
        out_specs=(vmem,) * 4,
        scratch_shapes=[
            pltpu.VMEM((2, tok, width), BF16),
            pltpu.VMEM((tok, columns), BF16),
            pltpu.VMEM((half, width), BF16),
            pltpu.VMEM((2, 4 * tok, width), BF16),
            pltpu.VMEM((4, 8, 128), jnp.int32),
            pltpu.VMEM((2, tok, half), BF16),
            pltpu.VMEM((tok, width), F32),
            pltpu.VMEM((tok, width), BF16),
            pltpu.VMEM((tok, width), BF16),
            pltpu.VMEM((2, tok, width), BF16),
            pltpu.VMEM((2, 2, tok, width), F32),
            pltpu.VMEM((2, 2, tok, width), BF16),
            pltpu.VMEM((2, 2, tok, width), BF16),
            pltpu.VMEM((3, tok, width), BF16),
            pltpu.VMEM((2, 4, tok, width), BF16),
            pltpu.VMEM((2, 2, 4, tok, columns // 4), BF16),
            pltpu.VMEM((2, 2, 4, tok, wide), BF16),
            pltpu.VMEM((rows_out, width), BF16),
            pltpu.VMEM((rows_out, width), BF16),
            pltpu.SMEM((1, 2), jnp.int32),
            dma((6,)),
            dma((2,)),
            dma((4,)),
            dma,
            dma,
            dma,
            dma((chunks,)),
            dma,
            dma((2, heads)),
            dma((3,)),
            dma((3, heads)),
            dma,
            dma,
            dma((4, 2)),
            dma,
            dma((4, 2)),
            dma,
            dma((4, 2)),
            dma,
            dma((heads,)),
            dma,
            dma((heads,)),
            dma,
            dma((heads,)),
            dma,
            dma((2, heads)),
            dma,
            dma((3, heads)),
            dma,
            dma((heads,)),
        ],
        compiler_params=pltpu.CompilerParams(
            collective_id=0, has_side_effects=True, vmem_limit_bytes=48 * 1024 * 1024
        ),
    )(valid, *[pltpu.with_memory_space_constraint(a, pltpu.HBM) for a in inputs])
    outs = write_out(outs)
    return outs[0][None], outs[1][None], outs[2][None], outs[3]


def solution(mesh):
    body = local
    if mesh.shape["seq"] == 4 and mesh.shape["dp"] == 2 and mesh.shape["head"] == 2:
        body = fused
    return jax.shard_map(
        body,
        mesh=mesh,
        in_specs=(
            P(("groups", "dp"), "seq", "head"),
            P(("groups", "dp"), "seq", "head"),
            P(("groups", "dp"), "seq", "head"),
            P(("groups", "dp"), "seq", None),
            P("dp", "head"),
            P("seq", None),
            P(("groups", "dp"), "seq"),
        ),
        out_specs=(
            P(("groups", "dp"), "seq", "head"),
            P(("groups", "dp"), "seq", "head"),
            P(("groups", "dp"), "seq", "head"),
            P(("groups", "seq", "dp"), "head"),
        ),
        check_vma=False,
    )
```

```python
import functools

import jax
import jax.numpy as jnp
from jax import lax
from jax.experimental import pallas as pl
from jax.experimental.pallas import tpu as pltpu
from jax.sharding import PartitionSpec as P

HEAD = 128


head_scale = 0.08838834764831845
masked_score = -1e30


def from_behind(value, axis, steps):
    count = lax.axis_size(axis)
    first, last = (max(0, -steps), min(count, count - steps))
    return lax.ppermute(value, axis, [(source, source + steps) for source in range(first, last)])


def split_heads(matrix):
    return matrix.reshape(matrix.shape[0], matrix.shape[1], -1, HEAD)


def local(queries, keys, values, out_grad, out_weight, pattern, valid):
    clip_count, row_count, width_dev = queries.shape
    levels = lax.axis_size("seq").bit_length() - 1
    positions = jnp.arange(row_count, dtype=jnp.int32)
    key_list = [keys]
    value_list = [values]
    visible_list = [positions[None, :] < valid]
    for level_index in range(levels):
        far_keys, far_values, far_valid = from_behind((keys, values, valid), "seq", 2**level_index)
        key_list.append(far_keys)
        value_list.append(far_values)
        visible_list.append((positions[None, :] < far_valid) & (pattern[0, level_index] > 0))
    key_heads = split_heads(jnp.concatenate(key_list, axis=1))
    value_heads = split_heads(jnp.concatenate(value_list, axis=1))
    visible = jnp.concatenate(visible_list, axis=1)
    query_heads = split_heads(queries)
    scores = (
        jnp.einsum("cqhd,ckhd->chqk", query_heads, key_heads, preferred_element_type=jnp.float32)
        * head_scale
    )
    scores = jnp.where(visible[:, None, None, :], scores, masked_score)
    row_max = jnp.max(scores, axis=-1, keepdims=True)
    log_total = row_max + jnp.log(jnp.sum(jnp.exp(scores - row_max), axis=-1, keepdims=True))
    probs_full = jnp.exp(scores - log_total)
    weights = probs_full.astype(jnp.bfloat16)
    attended = jnp.einsum(
        "chqk,ckhd->cqhd", weights, value_heads, preferred_element_type=jnp.float32
    ).astype(jnp.bfloat16)
    columns = out_grad
    grad_in = jnp.einsum(
        "cqe,eh->cqh",
        columns,
        lax.all_gather(out_weight, "dp", axis=0, tiled=True),
        preferred_element_type=jnp.float32,
    ).astype(jnp.bfloat16)
    grad_heads = split_heads(grad_in)
    row_delta = jnp.einsum(
        "cqhd,cqhd->chq", grad_heads.astype(jnp.float32), attended.astype(jnp.float32)
    )
    value_grad_all = jnp.einsum(
        "chqk,cqhd->ckhd", weights, grad_heads, preferred_element_type=jnp.float32
    )
    prob_grad = jnp.einsum(
        "cqhd,ckhd->chqk", grad_heads, value_heads, preferred_element_type=jnp.float32
    )
    score_grad = (probs_full * (prob_grad - row_delta[..., None])).astype(jnp.bfloat16)
    query_grad = (
        jnp.einsum("chqk,ckhd->cqhd", score_grad, key_heads, preferred_element_type=jnp.float32)
        * head_scale
    )
    key_grad_all = (
        jnp.einsum("chqk,cqhd->ckhd", score_grad, query_heads, preferred_element_type=jnp.float32)
        * head_scale
    )
    key_grad_all = key_grad_all.reshape(clip_count, -1, width_dev)
    value_grad_all = value_grad_all.reshape(clip_count, -1, width_dev)
    key_parts = [
        key_grad_all[:, set_index * row_count : (set_index + 1) * row_count]
        for set_index in range(levels + 1)
    ]
    value_parts = [
        value_grad_all[:, set_index * row_count : (set_index + 1) * row_count]
        for set_index in range(levels + 1)
    ]
    key_total = key_parts[0]
    value_total = value_parts[0]
    for level_index in range(levels):
        back_keys, back_values = (
            from_behind(
                key_parts[level_index + 1].astype(jnp.bfloat16), "seq", -(2**level_index)
            ).astype(jnp.float32),
            from_behind(
                value_parts[level_index + 1].astype(jnp.bfloat16), "seq", -(2**level_index)
            ).astype(jnp.float32),
        )
        key_total = key_total + back_keys
        value_total = value_total + back_values
    attended_rows = attended.reshape(clip_count, row_count, width_dev)
    columns = out_grad
    seq_total = lax.psum_scatter(
        jnp.einsum(
            "cqe,cqh->eh", columns, attended_rows, preferred_element_type=jnp.float32
        ).astype(jnp.bfloat16),
        "seq",
        scatter_dimension=0,
        tiled=True,
    )
    weight_grad = lax.psum_scatter(seq_total, "dp", scatter_dimension=0, tiled=True).astype(
        jnp.float32
    )
    query_out = query_grad.astype(jnp.bfloat16).reshape(clip_count, row_count, width_dev)
    return (
        query_out,
        key_total.astype(jnp.bfloat16),
        value_total.astype(jnp.bfloat16),
        weight_grad,
    )


MESH = pl.DeviceIdType.MESH
F32 = jnp.float32
BF16 = jnp.bfloat16
GRAD_CHUNK = 2 * HEAD


def dot_nn(a, b):
    return lax.dot_general(a, b, (((1,), (0,)), ((), ())), preferred_element_type=F32)


def dot_nt(a, b):
    return lax.dot_general(a, b, (((1,), (1,)), ((), ())), preferred_element_type=F32)


def dot_tn(a, b):
    return lax.dot_general(a, b, (((0,), (0,)), ((), ())), preferred_element_type=F32)


def attention(q, g, k, v, bias):
    scores = dot_nt(q, k) * head_scale + bias
    top = jnp.max(scores, axis=1, keepdims=True)
    raised = jnp.exp(scores - top)
    probs = raised * (1.0 / jnp.sum(raised, axis=1, keepdims=True))
    weights = probs.astype(BF16)
    attended = dot_nn(weights, v).astype(BF16)
    delta = jnp.sum(g.astype(F32) * attended.astype(F32), axis=1, keepdims=True)
    score_grad = (probs * (dot_nt(g, v) - delta)).astype(BF16)
    dq = (dot_nn(score_grad, k) * head_scale).astype(BF16)
    return attended, dq, dot_tn(score_grad, q) * head_scale, dot_tn(weights, g)


def kernel(
    rows_out,
    valid_ref,
    pattern_hbm,
    q_hbm,
    k_hbm,
    v_hbm,
    og_hbm,
    w_hbm,
    dq_ref,
    dk_ref,
    dv_ref,
    wg_ref,
    q_ref,
    og_ref,
    w_ref,
    kv,
    info,
    lhs,
    gacc,
    gsend,
    grecv,
    g_ref,
    acc,
    stage,
    back,
    outs,
    att,
    cols,
    pick,
    part,
    landed,
    pattern_ref,
    load_sem,
    info_send,
    info_recv,
    half_send,
    half_recv,
    gx_send,
    gx_recv,
    kv_send,
    kv_recv,
    edge_send,
    edge_recv,
    near_send,
    far_send,
    og_recv,
    x_send,
    x_recv,
    mate_send,
    mate_recv,
    att_send,
    att_recv,
    own_send,
    own_recv,
    fwd_send,
    fwd_recv,
    back_send,
    back_recv,
    res_send,
    res_recv,
    part_send,
    part_recv,
):
    s = lax.axis_index("seq")
    d = lax.axis_index("dp")
    h = lax.axis_index("head")
    tok, width = dq_ref.shape
    half = w_ref.shape[0]
    heads = width // HEAD
    seg = cols.shape[4]
    wide = pick.shape[4]
    mate = {"dp": 1 - d}
    part_rows = tok // 2

    def remote(src, dst, send, recv, device):
        return pltpu.make_async_remote_copy(
            src_ref=src, dst_ref=dst, send_sem=send, recv_sem=recv, device_id=device, device_id_type=MESH
        )

    def same(place, send, recv, device):
        return remote(place, place, send, recv, device)

    def cut(c):
        return pl.ds(c * HEAD, HEAD)

    def info_copy(block, target, slot):
        return same(info.at[block], info_send.at[slot], info_recv.at[block], {"seq": target})

    def half_copy():
        other = pl.multiple_of((1 - d) * half, half)
        return remote(og_ref.at[:, pl.ds(other, half)], lhs.at[1], half_send, half_recv, mate)

    def gx_copy(c):
        place = pl.ds(c * GRAD_CHUNK, GRAD_CHUNK)
        return remote(gsend.at[:, place], grecv.at[:, place], gx_send, gx_recv.at[c], mate)

    def kv_copy(which, c):
        first, count = ((0, 1), (1, 1), (0, 2))[which]
        place = kv.at[:, pl.ds(first * tok, count * tok), cut(c)]
        slot = 1 if which == 1 else 0
        return same(place, kv_send, kv_recv.at[slot, c], {"seq": 2})

    def edge_kv(block, c):
        place = kv.at[:, pl.ds(block * tok, tok), cut(c)]
        return same(place, edge_send.at[0], edge_recv.at[0, c], {"seq": 1 + block // 2})

    def edge_q(c):
        return remote(
            q_ref.at[0, :, cut(c)], q_ref.at[1, :, cut(c)], edge_send.at[1], edge_recv.at[1, c], {"seq": 2}
        )

    def edge_g(c):
        return remote(
            g_ref.at[0, :, cut(c)], g_ref.at[1, :, cut(c)], edge_send.at[2], edge_recv.at[2, c], {"seq": 2}
        )

    def edge_att(c):
        return same(att.at[d, 0, :, cut(c)], edge_send.at[1], edge_recv.at[1, c], {"seq": 1})

    def half_rows(row):
        return pl.ds(pl.multiple_of(row * part_rows, part_rows), part_rows)

    def own_columns(side, piece):
        return pl.ds((2 * side + (piece if side == 0 else 1 - piece)) * seg, seg)

    def og_copy(block, side, piece):
        sems = near_send if block // 2 == side else far_send
        return remote(
            og_ref.at[half_rows(h), own_columns(side, piece)],
            cols.at[d, piece, block, half_rows(h), :],
            sems,
            og_recv.at[block, piece],
            {"seq": 1 + side},
        )

    def x_copy(block, piece, mine):
        place = cols.at[d, piece, block, half_rows(h if mine else 1 - h), :]
        return same(place, x_send, x_recv.at[block, piece], {"head": 1 - h})

    def mate_copy(block, piece, clip):
        return same(cols.at[clip, piece, block], mate_send, mate_recv.at[block, piece], mate)

    def att_copy(pair, c):
        return same(
            att.at[d, pl.ds(2 * pair, 2), :, cut(c)], att_send, att_recv.at[c], {"seq": 2 - pair}
        )

    def own_copy(pair, c, clip):
        return same(att.at[clip, pl.ds(2 * pair, 2), :, cut(c)], own_send, own_recv.at[c], mate)

    def fwd_copy(pair, c, clip):
        return same(att.at[clip, pl.ds(2 * pair, 2), :, cut(c)], fwd_send, fwd_recv.at[c], mate)

    def back_copy(block, c, target):
        return remote(
            stage.at[:, block, :, cut(c)],
            back.at[:, block, :, cut(c)],
            back_send,
            back_recv.at[block, c],
            {"seq": target},
        )

    def res_copy(which, c):
        return remote(
            outs.at[which, :, cut(c)],
            (dq_ref, dk_ref, dv_ref)[which].at[:, cut(c)],
            res_send,
            res_recv.at[which, c],
            {"seq": 3},
        )

    def part_copy(c, target):
        return remote(part.at[:, cut(c)], landed.at[:, cut(c)], part_send, part_recv.at[c], {"seq": target})

    own_rows = pl.ds(pl.multiple_of(s * tok, tok), tok)
    loads = [
        pltpu.make_async_copy(k_hbm, kv.at[0, own_rows, :], load_sem.at[0]),
        pltpu.make_async_copy(v_hbm, kv.at[1, own_rows, :], load_sem.at[1]),
        pltpu.make_async_copy(og_hbm, og_ref, load_sem.at[2]),
        pltpu.make_async_copy(pattern_hbm, pattern_ref, load_sem.at[3]),
        pltpu.make_async_copy(q_hbm, q_ref.at[0], load_sem.at[4]),
        pltpu.make_async_copy(w_hbm, w_ref, load_sem.at[5]),
    ]

    barrier = pltpu.get_barrier_semaphore()
    for other in range(4):
        for mine in range(4):
            if mine != other and abs(mine - other) < 3:

                @pl.when(s == mine)
                def _(other=other):
                    pl.semaphore_signal(barrier, inc=1, device_id={"seq": other}, device_id_type=MESH)

    pl.semaphore_signal(barrier, inc=1, device_id=mate, device_id_type=MESH)
    pl.semaphore_signal(barrier, inc=1, device_id={"head": 1 - h}, device_id_type=MESH)
    for load in loads:
        load.start()
    loads[3].wait()
    line = lax.broadcasted_iota(jnp.int32, (8, 128), 0)
    info[s] = jnp.where(
        line == 0, valid_ref[0, 0], jnp.where(line == 1, pattern_ref[0, 0], pattern_ref[0, 1])
    )
    loads[0].wait()
    loads[1].wait()
    pl.semaphore_wait(barrier, 4 + lax.rem((s + 1) // 2, 2))

    @pl.when(s == 0)
    def _():
        for c in range(2):
            edge_kv(0, c).start()
        info_copy(0, 1, 0).start()
        info_copy(0, 2, 1).start()

    @pl.when(s == 1)
    def _():
        for c in range(2):
            kv_copy(1, c).start()
        info_copy(1, 2, 0).start()

    @pl.when(s == 3)
    def _():
        info_copy(3, 2, 0).start()
        edge_kv(3, 0).start()

    loads[2].wait()
    half_copy().start()

    @pl.when(s == 2)
    def _():
        for piece in (0, 1):
            og_copy(2, 0, piece).start()

    loads[4].wait()

    @pl.when(s == 3)
    def _():
        edge_q(0).start()
        og_copy(3, 0, 0).start()

    @pl.when(s == 0)
    def _():
        og_copy(0, 0, 0).start()
        og_copy(0, 1, 0).start()
        for c in (2, 3):
            edge_kv(0, c).start()

    lhs[0] = og_ref[:, pl.ds(pl.multiple_of(d * half, half), half)]
    loads[5].wait()
    half_copy().wait_recv()
    both = lhs[...].reshape(2 * tok, half)
    for c in range(width // GRAD_CHUNK):
        place = pl.ds(c * GRAD_CHUNK, GRAD_CHUNK)
        product = dot_nn(both, w_ref[:, place])
        gacc[:, place] = product[:tok]
        gsend[:, place] = product[tok:].astype(BF16)
        gx_copy(c).start()

    @pl.when(s == 1)
    def _():
        edge_kv(0, 0).wait_recv()
        kv_copy(0, 0).start()
        kv_copy(1, 2).start()
        edge_kv(0, 1).wait_recv()
        kv_copy(0, 1).start()
        og_copy(1, 1, 0).start()

    for block in (1, 2):

        @pl.when(s == block)
        def _(block=block):
            for piece in (0, 1):
                cols[d, piece, block] = og_ref[:, own_columns(block // 2, piece)]
                mate_copy(block, piece, d).start()

    for c in range(width // GRAD_CHUNK):
        place = pl.ds(c * GRAD_CHUNK, GRAD_CHUNK)
        gx_copy(c).wait_recv()
        g_ref[0, :, place] = (gacc[:, place] + grecv[:, place].astype(F32)).astype(BF16)

        @pl.when(s == 3)
        def _(c=c):
            for inner in (2 * c, 2 * c + 1):
                edge_g(inner).start()
            if c == 0:
                og_copy(3, 0, 1).start()
            if c == 1:
                og_copy(3, 1, 0).start()
            if c == 3:
                og_copy(3, 1, 1).start()
            for inner in (2 * c + 1, 2 * c + 2):
                if inner < heads:
                    edge_kv(3, inner).start()
                    edge_q(inner).start()

    lane = lax.broadcasted_iota(jnp.int32, (1, HEAD), 1)

    def shade(row_block, key_blocks):
        rows = []
        for key_block in key_blocks:
            seen = lane < info[key_block, 0:1, :]
            level = row_block - key_block
            if level:
                seen = jnp.logical_and(seen, info[row_block, level : level + 1, :] > 0)
            rows.append(jnp.where(seen, 0.0, masked_score))
        return jnp.concatenate(rows, axis=1)

    firsts = (0, wide - rows_out)

    def product(piece, place, count):
        return dot_tn(pick[piece].reshape(8 * tok, wide), att[:, :, :, place].reshape(8 * tok, count))

    def weigh_edge(role, c):
        own_copy(role - 1, c, 1 - d).wait_recv()
        fwd_copy(2 - role, c, 1 - d).wait_recv()
        full = product(0, cut(c), HEAD)
        for clip in (0, 1):

            @pl.when(d == clip)
            def _(clip=clip):
                part[:, cut(c)] = full[firsts[clip] : firsts[clip] + rows_out].astype(BF16)

        part_copy(c, 3 * (role - 1)).start()

    def weigh_own():
        for c in range(width // GRAD_CHUNK):
            place = pl.ds(c * GRAD_CHUNK, GRAD_CHUNK)
            full = product(1, place, GRAD_CHUNK)
            for clip in (0, 1):

                @pl.when(d == clip)
                def _(clip=clip):
                    wg_ref[:, place] = full[firsts[clip] : firsts[clip] + rows_out]

    def forward_rows(role, block, piece):
        og_copy(block, role - 1, piece).wait_recv()
        x_copy(block, piece, True).start()

    def forward_mate(role, block, piece):
        x_copy(block, piece, False).wait_recv()
        mate_copy(block, piece, d).start()

    def gather_columns(piece):
        for block in range(4):
            mate_copy(block, piece, 1 - d).wait_recv()
        first = pl.multiple_of(d * (seg - wide), HEAD)
        pick[piece] = cols[:, piece, :, :, pl.ds(first, wide)]

    @pl.when(s == 0)
    def _():
        bias = shade(0, (0,))
        for c in range(heads):
            hs = cut(c)
            attended, dq, dk, dv = attention(
                q_ref[0, :, hs], g_ref[0, :, hs], kv[0, :tok, hs], kv[1, :tok, hs], bias
            )
            att[d, 0, :, hs] = attended
            dq_ref[:, hs] = dq
            acc[0, 0, :, hs] = dk
            acc[1, 0, :, hs] = dv
            edge_att(c).start()
            if c + 4 < heads:
                edge_kv(0, c + 4).start()
            if c == 5:
                og_copy(0, 0, 1).start()
            if c == 7:
                og_copy(0, 1, 1).start()
        for c in range(heads):
            hs = cut(c)
            back_copy(0, c, 1).wait_recv()
            dk_ref[:, hs] = (acc[0, 0, :, hs] + back[0, 0, :, hs].astype(F32)).astype(BF16)
            dv_ref[:, hs] = (acc[1, 0, :, hs] + back[1, 0, :, hs].astype(F32)).astype(BF16)
            part_copy(c, 1).wait_recv()
            wg_ref[:, hs] = landed[:, hs].astype(F32)

    @pl.when(s == 1)
    def _():
        info_copy(0, 2, 0).wait_recv()
        bias = shade(1, (0, 1))
        for block in (2, 3, 0):
            forward_rows(1, block, 0)
        for c in range(heads + 2):
            if c < heads:
                hs = cut(c)
                attended, dq, dk, dv = attention(
                    q_ref[0, :, hs], g_ref[0, :, hs], kv[0, : 2 * tok, hs], kv[1, : 2 * tok, hs], bias
                )
                att[d, 1, :, hs] = attended
                dq_ref[:, hs] = dq
                for at, grad in ((0, dk), (1, dv)):
                    acc[at, 0, :, hs] = grad[:tok]
                    acc[at, 1, :, hs] = grad[tok:]
                if c + 2 < heads:
                    edge_kv(0, c + 2).wait_recv()
                    kv_copy(0 if c == 0 else 2, c + 2).start()
                edge_att(c).wait_recv()
                att_copy(0, c).start()
                own_copy(0, c, d).start()
                if c == 6:
                    og_copy(1, 1, 1).start()
            if c == 0:
                for block in (2, 3, 0):
                    forward_mate(1, block, 0)
            if c == 1:
                gather_columns(0)
                for block in (2, 3):
                    forward_rows(1, block, 1)
            if c == 2:
                for block in (2, 3):
                    forward_mate(1, block, 1)
            if c == 7:
                forward_rows(1, 0, 1)
            if c == 8:
                forward_mate(1, 0, 1)
            j = c - 2
            if 0 <= j < heads:
                hs = cut(j)
                att_copy(1, j).wait_recv()
                fwd_copy(1, j, d).start()
                back_copy(0, j, 1).wait_recv()
                stage[:, 0, :, hs] = (acc[:, 0, :, hs] + back[:, 0, :, hs].astype(F32)).astype(BF16)
                back_copy(0, j, 0).start()
                weigh_edge(1, j)
                back_copy(1, j, 1).wait_recv()
                total = acc[:, 1, :, hs] + back[:, 1, :, hs].astype(F32)
                dk_ref[:, hs] = total[0].astype(BF16)
                dv_ref[:, hs] = total[1].astype(BF16)
        gather_columns(1)
        weigh_own()

    @pl.when(s == 2)
    def _():
        for block in (0, 1, 3):
            info_copy(block, 2, 0).wait_recv()
        bias_own = shade(2, (0, 1, 2))
        bias_edge = shade(3, (1, 2, 3))
        for c in range(heads + 3):
            if c < heads:
                hs = cut(c)
                if c < 3:
                    kv_copy(1, c).wait_recv()
                    kv_copy(0, c).wait_recv()
                else:
                    kv_copy(2, c).wait_recv()
                edge_kv(3, c).wait_recv()
                edge_q(c).wait_recv()
                edge_g(c).wait_recv()
                own = attention(
                    q_ref[0, :, hs], g_ref[0, :, hs], kv[0, : 3 * tok, hs], kv[1, : 3 * tok, hs], bias_own
                )
                edge = attention(
                    q_ref[1, :, hs], g_ref[1, :, hs], kv[0, tok:, hs], kv[1, tok:, hs], bias_edge
                )
                att[d, 2, :, hs] = own[0]
                att[d, 3, :, hs] = edge[0]
                att_copy(1, c).start()
                for at in (0, 1):
                    stage[at, 0, :, hs] = own[2 + at][:tok].astype(BF16)
                    stage[at, 1, :, hs] = (own[2 + at][tok : 2 * tok] + edge[2 + at][:tok]).astype(BF16)
                back_copy(0, c, 1).start()
                back_copy(1, c, 1).start()
                own_copy(1, c, d).start()
                outs[0, :, hs] = edge[1]
                for at in (0, 1):
                    outs[1 + at, :, hs] = edge[2 + at][2 * tok :].astype(BF16)
                for which in range(3):
                    res_copy(which, c).start()
                dq_ref[:, hs] = own[1]
                dk_ref[:, hs] = (own[2][2 * tok :] + edge[2][tok : 2 * tok]).astype(BF16)
                dv_ref[:, hs] = (own[3][2 * tok :] + edge[3][tok : 2 * tok]).astype(BF16)
            if c == 1:
                for block in (3, 0, 1):
                    forward_rows(2, block, 0)
            if c == 2:
                for block in (3, 0, 1):
                    forward_mate(2, block, 0)
            if c == 3:
                gather_columns(0)
            j = c - 2
            if 0 <= j < heads:
                att_copy(0, j).wait_recv()
                fwd_copy(0, j, d).start()
            if 0 <= c - 3 < heads:
                weigh_edge(2, c - 3)
            if c == heads - 1:
                for block in (0, 1, 3):
                    forward_rows(2, block, 1)
            if c == heads:
                for block in (0, 1, 3):
                    forward_mate(2, block, 1)
        gather_columns(1)
        weigh_own()

    @pl.when(s == 3)
    def _():
        for c in range(heads):
            for which in range(3):
                res_copy(which, c).wait_recv()
            part_copy(c, 3).wait_recv()
            wg_ref[:, cut(c)] = landed[:, cut(c)].astype(F32)

    def all_sent(place, send):
        remote(place, place, send, half_recv, mate).wait_send()

    half_copy().wait_send()
    all_sent(gsend, gx_send)
    half_og = og_ref.at[half_rows(0), pl.ds(0, 2 * seg)]

    @pl.when(s == 0)
    def _():
        for target in (1, 2):
            info_copy(0, target, target - 1).wait_send()
        all_sent(kv.at[:, pl.ds(0, tok), :], edge_send.at[0])
        all_sent(att.at[d, 0], edge_send.at[1])
        all_sent(half_og, near_send)
        all_sent(half_og, far_send)

    @pl.when(s == 3)
    def _():
        info_copy(3, 2, 0).wait_send()
        all_sent(kv.at[:, pl.ds(3 * tok, tok), :], edge_send.at[0])
        all_sent(q_ref.at[0], edge_send.at[1])
        all_sent(g_ref.at[0], edge_send.at[2])
        all_sent(half_og, near_send)
        all_sent(half_og, far_send)

    for role in (1, 2):

        @pl.when(s == role)
        def _(role=role):
            all_sent(half_og, far_send)
            all_sent(cols.at[d, :, pl.ds(0, 3), half_rows(0), :], x_send)
            all_sent(cols.at[d], mate_send)
            pair = att.at[d, pl.ds(2 * (role - 1), 2)]
            all_sent(pair, att_send)
            all_sent(pair, own_send)
            all_sent(pair, fwd_send)
            all_sent(part, part_send)
            if role == 1:
                info_copy(1, 2, 0).wait_send()
                all_sent(kv.at[:, pl.ds(0, 2 * tok), :], kv_send)
                all_sent(stage.at[:, 0], back_send)
            else:
                all_sent(stage, back_send)
                all_sent(outs, res_send)


def out_kernel(*refs):
    count = len(refs) // 2
    sems = refs[-1]
    copies = [pltpu.make_async_copy(refs[i], refs[count + i], sems.at[i]) for i in range(count)]
    for copy in copies:
        copy.start()
    for copy in copies:
        copy.wait()


def write_out(arrays):
    return pl.pallas_call(
        out_kernel,
        out_shape=tuple(jax.ShapeDtypeStruct(a.shape, a.dtype) for a in arrays),
        in_specs=[pl.BlockSpec(memory_space=pltpu.VMEM)] * len(arrays),
        out_specs=(pl.BlockSpec(memory_space=pltpu.HBM),) * len(arrays),
        scratch_shapes=[pltpu.SemaphoreType.DMA((len(arrays),))],
        compiler_params=pltpu.CompilerParams(vmem_limit_bytes=4 * 1024 * 1024),
    )(*arrays)


def fused(queries, keys, values, out_grad, out_weight, pattern, valid):
    _, tok, width = queries.shape
    columns = out_grad.shape[2]
    rows_out = columns // 8
    half = out_weight.shape[0]
    heads = width // HEAD
    chunks = width // GRAD_CHUNK
    wide = -(-rows_out // HEAD) * HEAD
    vmem = pl.BlockSpec(memory_space=pltpu.VMEM)
    hbm = pl.BlockSpec(memory_space=pltpu.HBM)
    smem = pl.BlockSpec(memory_space=pltpu.SMEM)
    dma = pltpu.SemaphoreType.DMA
    rows_bf = jax.ShapeDtypeStruct((tok, width), BF16)
    inputs = (pattern, queries[0], keys[0], values[0], out_grad[0], out_weight)
    outs = pl.pallas_call(
        functools.partial(kernel, rows_out),
        out_shape=(rows_bf, rows_bf, rows_bf, jax.ShapeDtypeStruct((rows_out, width), F32)),
        in_specs=[smem] + [hbm] * 6,
        out_specs=(vmem,) * 4,
        scratch_shapes=[
            pltpu.VMEM((2, tok, width), BF16),
            pltpu.VMEM((tok, columns), BF16),
            pltpu.VMEM((half, width), BF16),
            pltpu.VMEM((2, 4 * tok, width), BF16),
            pltpu.VMEM((4, 8, 128), jnp.int32),
            pltpu.VMEM((2, tok, half), BF16),
            pltpu.VMEM((tok, width), F32),
            pltpu.VMEM((tok, width), BF16),
            pltpu.VMEM((tok, width), BF16),
            pltpu.VMEM((2, tok, width), BF16),
            pltpu.VMEM((2, 2, tok, width), F32),
            pltpu.VMEM((2, 2, tok, width), BF16),
            pltpu.VMEM((2, 2, tok, width), BF16),
            pltpu.VMEM((3, tok, width), BF16),
            pltpu.VMEM((2, 4, tok, width), BF16),
            pltpu.VMEM((2, 2, 4, tok, columns // 4), BF16),
            pltpu.VMEM((2, 2, 4, tok, wide), BF16),
            pltpu.VMEM((rows_out, width), BF16),
            pltpu.VMEM((rows_out, width), BF16),
            pltpu.SMEM((1, 2), jnp.int32),
            dma((6,)),
            dma((2,)),
            dma((4,)),
            dma,
            dma,
            dma,
            dma((chunks,)),
            dma,
            dma((2, heads)),
            dma((3,)),
            dma((3, heads)),
            dma,
            dma,
            dma((4, 2)),
            dma,
            dma((4, 2)),
            dma,
            dma((4, 2)),
            dma,
            dma((heads,)),
            dma,
            dma((heads,)),
            dma,
            dma((heads,)),
            dma,
            dma((2, heads)),
            dma,
            dma((3, heads)),
            dma,
            dma((heads,)),
        ],
        compiler_params=pltpu.CompilerParams(
            collective_id=0, has_side_effects=True, vmem_limit_bytes=48 * 1024 * 1024
        ),
    )(valid, *[pltpu.with_memory_space_constraint(a, pltpu.HBM) for a in inputs])
    outs = write_out(outs)
    return outs[0][None], outs[1][None], outs[2][None], outs[3]


def solution(mesh):
    body = local
    if mesh.shape["seq"] == 4 and mesh.shape["dp"] == 2 and mesh.shape["head"] == 2:
        body = fused
    return jax.shard_map(
        body,
        mesh=mesh,
        in_specs=(
            P(("groups", "dp"), "seq", "head"),
            P(("groups", "dp"), "seq", "head"),
            P(("groups", "dp"), "seq", "head"),
            P(("groups", "dp"), "seq", None),
            P("dp", "head"),
            P("seq", None),
            P(("groups", "dp"), "seq"),
        ),
        out_specs=(
            P(("groups", "dp"), "seq", "head"),
            P(("groups", "dp"), "seq", "head"),
            P(("groups", "dp"), "seq", "head"),
            P(("groups", "seq", "dp"), "head"),
        ),
        check_vma=False,
    )
```
